512 devices in a mesh: space: 64 (over z, x_hi, core), scen: 8 (over x_lo, y).
Axes of the slice: x: 4 (x_hi: 2, x_lo: 2; x = x_hi * 2 + x_lo), y: 4, z: 16, core: 2. Of those that a mesh axis runs over, the one named last changes fastest.
Arguments:
- dwell_map: bfloat16 [16384, 1024], P('space', 'scen'), may hold values from 0 to 1
- target_map: bfloat16 [16384, 1024], P('space'), may hold values from -6 to 6
- bound_mask: int32 [16384, 1024], P('space', 'scen'), may hold values 0 or 1
- offsets: int32 [16, 2], replicated, may hold values from -32 to 32, as said below
- rate_index: int32 [16, 1], replicated, may hold values from 0 to 3
- rate_table: float32 [4], replicated, may hold values from 0.5 to 2
- row_kernels: bfloat16 [4, 63], replicated, may hold values from -0.75 to 0.75
- col_kernels: bfloat16 [4, 63], replicated, may hold values from -0.75 to 0.75
Outputs:
- dwell_next: bfloat16 [16384, 1024], P('space', 'scen')
The draws below stay inside these ranges and needn't reach their ends.
Inputs may be any that keep to these rules, and one draw needn't show every extreme that they name: `offsets`: each entry lies between -32 and 32; in each column some scenario has 32 and another -32. `rate_index`: every level is used by some scenario.
All inputs are finite; a program needn't handle non-finite values. No bound on the sum of `bound_mask` on one device may be relied on, other than what follows from the above.
Results may differ from the reference program's by a relative error of at most 0.014.
Values may be sent and summed in bfloat16 or wider, within the bound.
A program may use at most 64 MiB of HBM per device.

```python
import math
import jax
import jax.numpy as jnp
from jax import lax

S_DEV = 2
KTAPS = 63
REACH = 32
NRATE = 4
SCEN = 16
H = 16384
W = 1024
N_SCEN = 8


def draw_offsets(key, part):
    first_key = jax.random.fold_in(key, 11)
    second_key = jax.random.fold_in(key, 12)
    base = jax.random.randint(first_key, (SCEN, 2), -REACH, REACH + 1)
    order = jax.random.permutation(second_key, SCEN)
    base = base.at[order[0], 0].set(REACH)
    base = base.at[order[1], 0].set(-REACH)
    base = base.at[order[2], 1].set(REACH)
    base = base.at[order[3], 1].set(-REACH)
    return base.astype(jnp.int32)


def plant(result, rng, smallest, largest):
    place = [jax.random.randint(jax.random.fold_in(rng, axis), (), 0, length) for axis, length in enumerate(result.shape)]
    longest = result.shape.index(max(result.shape))
    neighbour = place[:longest] + [(place[longest] + 1) % result.shape[longest]] + place[longest + 1:]
    return result.at[tuple(place)].set(smallest).at[tuple(neighbour)].set(largest)


def steps_of(rng, shape, cuts, low, high):
    loudness = 1.0
    for dim, blocks in cuts:
        draws = jax.random.uniform(jax.random.fold_in(jax.random.fold_in(rng, 6), dim), (blocks,), jnp.float32, low / len(cuts), high / len(cuts))
        loudness = loudness * jnp.repeat(jnp.exp(draws), shape[dim] // blocks).reshape((-1,) + (1,) * (len(shape) - 1 - dim))
    return loudness


def different_ones(rng, rows, count, top, lift):
    sequence = jax.random.permutation(jax.random.fold_in(rng, 1), count)
    favour = sequence
    for power in range(3):
        favour = favour * favour // count
    favour = favour * lift // count
    tickets = jax.random.randint(jax.random.fold_in(rng, 2), (rows, count), 0, 4096) + favour
    sure = jax.random.permutation(jax.random.fold_in(rng, 3), rows)[jnp.arange(count) % rows]
    tickets = jnp.where(jnp.arange(rows)[:, None] == sure[None, :], 1 << 14, tickets)
    priority = tickets * count + jnp.arange(count)
    return lax.top_k(priority.astype(jnp.int32), top)[1].astype(jnp.int32)


def bell_draw(key, extent, deviation, most, cuts=(), kind=jnp.bfloat16):
    values = jax.random.normal(key, extent, jnp.float32) * deviation
    if len(cuts) > 0:
        values = steps_of(key, extent, cuts, -0.22, 0.18) * values
    return jnp.clip(values, min=-most, max=most).astype(kind)


def setup_inputs(seed: int = 0) -> dict:
    seeds = jax.random.split(jax.random.key(seed), 9)
    return {
        "dwell_map": jnp.clip(1.0 * jax.random.uniform(seeds[0], (H, W), jnp.float32) ** steps_of(seeds[0], (H, W), ((0, 64), (1, 8)), -0.2, 0.2), 0.0, 1.0).astype(jnp.bfloat16),
        "target_map": bell_draw(seeds[1], (H, W), 1.0, 6.0, ((0, 64),)),
        "bound_mask": plant((jax.random.randint(seeds[2], (H, W), 0, 2) < 1).astype(jnp.int32), jax.random.fold_in(seeds[2], 1), 0, 1),
        "offsets": draw_offsets(jax.random.fold_in(seeds[8], 71), 0),
        "rate_index": different_ones(seeds[4], SCEN, NRATE, 1, 0),
        "rate_table": jnp.clip(jnp.exp(jax.random.uniform(seeds[5], (NRATE,), jnp.float32, math.log(0.5), math.log(2.0))), 0.5, 2.0),
        "row_kernels": bell_draw(seeds[6], (NRATE, KTAPS), KTAPS ** -0.5, 0.75),
        "col_kernels": bell_draw(seeds[7], (NRATE, KTAPS), KTAPS ** -0.5, 0.75),
    }


step_size = 1.0


def band_line(kernel, start_at, row_count, col_count):
    kernel_line = jnp.zeros((col_count + 1,), kernel.dtype)
    kernel_line = lax.dynamic_update_slice(kernel_line, kernel, (start_at,))
    return jnp.tile(kernel_line, row_count)[: row_count * col_count].reshape(row_count, col_count)


def pick_block(length):
    return 128 if length % 128 == 0 else 32


def along_rows(values, kernel, start_at):
    length = values.shape[0]
    col_block = pick_block(length)
    padded = jnp.pad(values, ((col_block, col_block), (0, 0)))
    pieces = [padded[piece * col_block: piece * col_block + length].reshape(length // col_block, col_block, -1) for piece in range(3)]
    stacked = jnp.concatenate(pieces, axis=1)
    matrix = band_line(kernel, start_at + col_block, col_block, 3 * col_block)
    product = jnp.einsum('cy,nym->ncm', matrix, stacked, precision=lax.Precision.HIGHEST)
    return product.reshape(length, -1)


def along_cols(values, kernel, start_at):
    length = values.shape[1]
    row_count = values.shape[0]
    col_block = pick_block(length)
    padded = jnp.pad(values, ((0, 0), (col_block, col_block)))
    pieces = [padded[:, piece * col_block: piece * col_block + length].reshape(row_count, length // col_block, col_block) for piece in range(3)]
    stacked = jnp.concatenate(pieces, axis=2)
    matrix = band_line(kernel, start_at + col_block, col_block, 3 * col_block)
    product = jnp.einsum('rny,cy->rnc', stacked, matrix, precision=lax.Precision.HIGHEST)
    return product.reshape(row_count, length)


def reference(dwell_map, target_map, bound_mask, offsets, rate_index, rate_table, row_kernels, col_kernels):
    radius = (KTAPS - 1) // 2
    dwell_f = dwell_map.astype(jnp.float32)
    target_f = target_map.astype(jnp.float32)

    def scenario(index):
        level = rate_index[index, 0]
        rate_now = rate_table[level]
        row_taps = row_kernels[level].astype(jnp.float32)
        col_taps = col_kernels[level].astype(jnp.float32)
        shift_rows = offsets[index, 0]
        shift_cols = offsets[index, 1]
        forward = along_rows(dwell_f, row_taps, -radius - shift_rows).astype(jnp.bfloat16)
        forward = lax.optimization_barrier(forward).astype(jnp.float32)
        removal = rate_now * along_cols(forward, col_taps, -radius - shift_cols)
        misfit = lax.optimization_barrier((removal - target_f).astype(jnp.bfloat16)).astype(jnp.float32)
        back_cols = along_cols(misfit, col_taps[::-1], -radius + shift_cols).astype(jnp.bfloat16)
        back_cols = lax.optimization_barrier(back_cols).astype(jnp.float32)
        adjoint = along_rows(back_cols, row_taps[::-1], -radius + shift_rows)
        return (rate_now / SCEN) * adjoint

    def group(summed, device):
        group_sum = jnp.zeros(dwell_map.shape, jnp.float32)
        for member in range(S_DEV):
            group_sum = group_sum + scenario(device * S_DEV + member)
        rounded = lax.optimization_barrier(group_sum.astype(jnp.bfloat16)).astype(jnp.float32)
        return summed + rounded, None

    gradient, unused = lax.scan(group, jnp.zeros(dwell_map.shape, jnp.float32), jnp.arange(N_SCEN, dtype=jnp.int32))
    stepped = dwell_f - step_size * gradient
    return jnp.where(bound_mask == 1, jnp.maximum(stepped, 0.0), stepped).astype(jnp.bfloat16)
```

```python
import functools

import jax
import jax.numpy as jnp
from jax import lax
from jax.experimental import pallas as pl
from jax.experimental.pallas import tpu as pltpu
from jax.sharding import PartitionSpec as P

MESH = pl.DeviceIdType.MESH
F32 = jnp.float32
BF16 = jnp.bfloat16

TAPS = 63
RADIUS = 31
ROWS = 256
COLS = 128
RIM = 64
RING = 256
OUT = 320
NRATE = 4
SCEN = 16
STEP_SIZE = 1.0
CHUNK = 16


def lanes(shape):
    return lax.broadcasted_iota(jnp.int32, shape, len(shape) - 1)


def kernel(
    n_space,
    n_scen,
    dwell_hbm,
    target_hbm,
    off_s,
    level_s,
    rate_s,
    off_v,
    level_v,
    row_taps,
    col_taps,
    grad_ref,
    dwell_x,
    pack_l,
    pack_r,
    recv_l,
    recv_r,
    t_own,
    t_top,
    t_bot,
    wide,
    taps8,
    row_fwd,
    col_mat,
    row_adj,
    count,
    t_sum,
    along,
    back,
    send_sem,
    recv_sem,
    load_sem,
):
    sp = lax.axis_index("space")
    sc = lax.axis_index("scen")
    up, down = (sp + n_space - 1) % n_space, (sp + 1) % n_space
    left, right = (sc + n_scen - 1) % n_scen, (sc + 1) % n_scen
    core = sp % 2
    other = (sc + n_scen // 2) % n_scen
    up_sc = jnp.where(core == 0, other, sc)
    down_sc = jnp.where(core == 0, sc, other)

    def first_tile(c):
        return jnp.minimum(jnp.maximum(c - 1, 0), n_scen - 3)

    def window(c):
        return pl.ds(pl.multiple_of(first_tile(c) * COLS, COLS), 3 * COLS)

    peers = (
        (up, sc),
        (down, sc),
        (sp, left),
        (sp, right),
        (up, left),
        (up, right),
        (down, left),
        (down, right),
        (up, up_sc),
        (down, down_sc),
    )
    barrier = pltpu.get_barrier_semaphore()
    for peer in peers:
        pl.semaphore_signal(barrier, inc=1, device_id=peer, device_id_type=MESH)

    load_dwell = pltpu.make_async_copy(
        dwell_hbm, dwell_x.at[RIM : RIM + ROWS, 0:COLS], load_sem.at[0]
    )
    load_target = pltpu.make_async_copy(target_hbm.at[:, window(sc)], t_own, load_sem.at[1])
    load_dwell.start()
    load_target.start()
    load_dwell.wait()

    low = lanes((32, COLS)) < RIM
    for g in range(4):
        base = RIM + 64 * g
        first = dwell_x[base : base + 32, 0:COLS].astype(F32)
        second = pltpu.roll(dwell_x[base + 32 : base + 64, 0:COLS].astype(F32), RIM, 1)
        pack_l[32 * g : 32 * g + 32, :] = jnp.where(low, first, second).astype(BF16)
        pack_r[32 * g : 32 * g + 32, :] = jnp.where(low, second, first).astype(BF16)

    pl.semaphore_wait(barrier, len(peers))

    sides = (
        (pack_l, recv_r.at[32:160]),
        (pack_r, recv_l.at[32:160]),
        (pack_l.at[0:32], recv_r.at[160:192]),
        (pack_r.at[0:32], recv_l.at[160:192]),
        (pack_l.at[96:128], recv_r.at[0:32]),
        (pack_r.at[96:128], recv_l.at[0:32]),
    )
    pairs = (
        (dwell_hbm.at[0:RIM], dwell_x.at[RIM + ROWS : RIM + ROWS + RIM, 0:COLS]),
        (dwell_hbm.at[ROWS - RIM : ROWS], dwell_x.at[0:RIM, 0:COLS]),
        *sides,
        (target_hbm.at[0:RIM, window(up_sc)], t_bot),
        (target_hbm.at[ROWS - RIM : ROWS, window(down_sc)], t_top),
    )
    copies = [
        pltpu.make_async_remote_copy(
            src_ref=src,
            dst_ref=dst,
            send_sem=send_sem.at[k],
            recv_sem=recv_sem.at[k],
            device_id=peers[k],
            device_id_type=MESH,
        )
        for k, (src, dst) in enumerate(pairs)
    ]
    for k in (2, 3, 4, 5, 6, 7, 0, 1, 8, 9):
        copies[k].start()

    has_up = jnp.where(sp > 0, 1.0, 0.0).astype(F32)
    has_down = jnp.where(sp < n_space - 1, 1.0, 0.0).astype(F32)
    has_left = jnp.where(sc > 0, 1.0, 0.0).astype(F32)
    has_right = jnp.where(sc < n_scen - 1, 1.0, 0.0).astype(F32)

    taps8[...] = jnp.zeros_like(taps8)
    taps8[0:NRATE, 0:TAPS] = row_taps[...].astype(F32)
    taps8[4 : 4 + NRATE, 0:TAPS] = col_taps[...].astype(F32)
    taps = taps8[...]
    flip = jnp.where(
        lax.broadcasted_iota(jnp.int32, (RING, RING), 0) + lanes((RING, RING)) == TAPS - 1, 1.0, 0.0
    ).astype(BF16)
    reversed_taps = jnp.dot(taps.astype(BF16), flip, preferred_element_type=F32)

    def toeplitz(line, count_, first):
        return pltpu.roll(
            jnp.broadcast_to(line, (count_, RING)), first % RING, 1, stride=1, stride_axis=0
        ).astype(BF16)

    for q in range(NRATE):
        row_fwd[0, 160 * q : 160 * q + 160, :] = toeplitz(taps[q : q + 1], 160, 1)
        row_fwd[1, 160 * q : 160 * q + 160, :] = toeplitz(taps[q : q + 1], 160, 33)
        col_mat[q] = toeplitz(taps[4 + q : 5 + q], RING, -RADIUS)
        row_adj[:, RING * q : RING * q + RING] = toeplitz(reversed_taps[q : q + 1], 128, 1)

    offs = off_v[...]
    row_at = sp * ROWS + lax.broadcasted_iota(jnp.int32, (OUT, SCEN), 0) - 32 + offs[0:1, :]
    row_in = jnp.where((row_at >= 0) & (row_at < n_space * ROWS), 1.0, 0.0).astype(BF16)
    ring_at = lax.broadcasted_iota(jnp.int32, (RING, SCEN), 0)
    col_at = jnp.where(ring_at < COLS + RIM, ring_at, ring_at - RING) + sc * COLS + offs[1:2, :]
    col_in = jnp.where((col_at >= 0) & (col_at < n_scen * COLS), 1.0, 0.0)
    levels = level_v[...]
    for q in range(NRATE):
        mine = jnp.where(levels == q, 1.0, 0.0)
        seen = lax.dot_general(
            row_in, (col_in * mine).astype(BF16), (((1,), (1,)), ((), ())), preferred_element_type=F32
        )
        rate = rate_s[q]
        count[q] = seen * (rate * rate * (1.0 / SCEN))

    at = sc - first_tile(sc)
    ring_low = lanes((1, COLS)) < RIM
    side_ok = jnp.where(ring_low, has_right, has_left)

    def to_ring(ref, rows):
        own = ref[rows, pl.ds(pl.multiple_of(at * COLS, COLS), COLS)].astype(F32)
        after = ref[rows, pl.ds(pl.multiple_of(jnp.minimum(at + 1, 2) * COLS, COLS), COLS)].astype(F32)
        before = ref[rows, pl.ds(pl.multiple_of(jnp.maximum(at - 1, 0) * COLS, COLS), COLS)].astype(F32)
        return own, jnp.where(ring_low, after, before) * side_ok

    load_target.wait()
    own, side = to_ring(t_own, slice(0, ROWS))
    wide[0, RIM : RIM + ROWS, :] = own
    wide[1, RIM : RIM + ROWS, :] = side

    shift_rows = [off_s[0, s] for s in range(SCEN)]
    shift_cols = [lax.rem(RING - off_s[1, s], RING) for s in range(SCEN)]
    weights = [
        [jnp.where(level_s[0, s] == q, rate_s[q] * (1.0 / SCEN), 0.0) for q in range(NRATE)]
        for s in range(SCEN)
    ]

    def target_rows(c, carry):
        begin = c * CHUNK
        sums = [jnp.zeros((CHUNK, RING), F32) for _ in range(NRATE)]
        for s in range(SCEN):
            start = begin + 32 + shift_rows[s]
            part = jnp.concatenate([wide[side_, pl.ds(start, CHUNK), :] for side_ in range(2)], axis=1)
            part = pltpu.roll(part, shift_cols[s], 1)
            sums = [acc + weights[s][q] * part for q, acc in enumerate(sums)]
        for q in range(NRATE):
            t_sum[q, pl.ds(pl.multiple_of(begin, CHUNK), CHUNK), :] = sums[q]
        return carry

    lax.fori_loop(64 // CHUNK, 256 // CHUNK, target_rows, 0)

    for copy in copies[8:]:
        copy.wait()
    own, side = to_ring(t_top, slice(0, RIM))
    wide[0, 0:RIM, :] = own * has_up
    wide[1, 0:RIM, :] = side * has_up
    own, side = to_ring(t_bot, slice(0, RIM))
    wide[0, RIM + ROWS :, :] = own * has_down
    wide[1, RIM + ROWS :, :] = side * has_down
    lax.fori_loop(0, 64 // CHUNK, target_rows, 0)
    lax.fori_loop(256 // CHUNK, OUT // CHUNK, target_rows, 0)

    for copy in copies[:8]:
        copy.wait()

    dwell_x[0:RIM, 0:COLS] = (dwell_x[0:RIM, 0:COLS].astype(F32) * has_up).astype(BF16)
    dwell_x[RIM + ROWS :, 0:COLS] = (dwell_x[RIM + ROWS :, 0:COLS].astype(F32) * has_down).astype(BF16)
    for g in range(6):
        ok = side_ok
        if g == 0:
            ok = ok * has_up
        if g == 5:
            ok = ok * has_down
        after = recv_r[32 * g : 32 * g + 32, :].astype(F32)
        before = recv_l[32 * g : 32 * g + 32, :].astype(F32)
        first = jnp.where(low, after, before) * ok
        second = pltpu.roll(jnp.where(low, before, after), RIM, 1) * ok
        dwell_x[64 * g : 64 * g + 32, COLS:RING] = first.astype(BF16)
        dwell_x[64 * g + 32 : 64 * g + 64, COLS:RING] = second.astype(BF16)

    for half in range(2):
        product = jnp.dot(
            row_fwd[half], dwell_x[128 * half : 128 * half + 256, :], preferred_element_type=F32
        ).astype(BF16)
        for q in range(NRATE):
            along[q, 160 * half : 160 * half + 160, :] = product[160 * q : 160 * q + 160]

    for q in range(NRATE):
        base = lax.dot_general(
            along[q], col_mat[q], (((1,), (1,)), ((), ())), preferred_element_type=F32
        )
        misfit = (count[q] * base - t_sum[q]).astype(BF16)
        product = jnp.dot(misfit, col_mat[q, :, 0:COLS], preferred_element_type=F32).astype(BF16)
        back[RING * q : RING * q + 256, 0:COLS] = product[0:256]
        back[RING * q : RING * q + 192, COLS:RING] = product[128:OUT]
        back[RING * q + 192 : RING * q + 256, COLS:RING] = jnp.zeros((64, COLS), BF16)

    grad = jnp.dot(row_adj[...], back[...], preferred_element_type=F32)
    grad_ref[0:128, :] = grad[:, 0:COLS]
    grad_ref[128:256, :] = grad[:, COLS:RING]


def tile_step(n_space, n_scen, dwell, target, bound, offsets, level, rates, row_kernels, col_kernels):
    offsets, level = offsets.T, level.T
    vmem = pl.BlockSpec(memory_space=pltpu.VMEM)
    smem = pl.BlockSpec(memory_space=pltpu.SMEM)
    far = pl.BlockSpec(memory_space=pltpu.HBM)
    gradient = pl.pallas_call(
        functools.partial(kernel, n_space, n_scen),
        out_shape=jax.ShapeDtypeStruct((ROWS, COLS), F32),
        in_specs=[far, far, smem, smem, smem, vmem, vmem, vmem, vmem],
        out_specs=vmem,
        scratch_shapes=[
            pltpu.VMEM((384, RING), BF16),
            pltpu.VMEM((128, COLS), BF16),
            pltpu.VMEM((128, COLS), BF16),
            pltpu.VMEM((192, COLS), BF16),
            pltpu.VMEM((192, COLS), BF16),
            pltpu.VMEM((ROWS, 3 * COLS), BF16),
            pltpu.VMEM((RIM, 3 * COLS), BF16),
            pltpu.VMEM((RIM, 3 * COLS), BF16),
            pltpu.VMEM((2, 384, COLS), F32),
            pltpu.VMEM((8, RING), F32),
            pltpu.VMEM((2, NRATE * 160, RING), BF16),
            pltpu.VMEM((NRATE, RING, RING), BF16),
            pltpu.VMEM((128, NRATE * RING), BF16),
            pltpu.VMEM((NRATE, OUT, RING), F32),
            pltpu.VMEM((NRATE, OUT, RING), F32),
            pltpu.VMEM((NRATE, OUT, RING), BF16),
            pltpu.VMEM((NRATE * RING, RING), BF16),
            pltpu.SemaphoreType.DMA((10,)),
            pltpu.SemaphoreType.DMA((10,)),
            pltpu.SemaphoreType.DMA((2,)),
        ],
        compiler_params=pltpu.CompilerParams(collective_id=0, vmem_limit_bytes=63 * 1024 * 1024),
    )(dwell, target, offsets, level, rates, offsets, level, row_kernels, col_kernels)
    stepped = dwell.astype(F32) - STEP_SIZE * gradient
    return jnp.where(bound == 1, jnp.maximum(stepped, 0.0), stepped).astype(BF16)


def solution(mesh):
    return jax.shard_map(
        functools.partial(tile_step, mesh.shape["space"], mesh.shape["scen"]),
        mesh=mesh,
        in_specs=(P("space", "scen"), P("space", None), P("space", "scen"), P(), P(), P(), P(), P()),
        out_specs=P("space", "scen"),
        check_vma=False,
    )
```

```python
import functools

import jax
import jax.numpy as jnp
from jax import lax
from jax.experimental import pallas as pl
from jax.experimental.pallas import tpu as pltpu
from jax.sharding import PartitionSpec as P

MESH = pl.DeviceIdType.MESH
F32 = jnp.float32
BF16 = jnp.bfloat16

TAPS = 63
RADIUS = 31
ROWS = 256
COLS = 128
RIM = 64
RING = 256
OUT = 320
NRATE = 4
SCEN = 16
STEP_SIZE = 1.0
CHUNK = 16


def lanes(shape):
    return lax.broadcasted_iota(jnp.int32, shape, len(shape) - 1)


def kernel(
    n_space,
    n_scen,
    dwell_hbm,
    target_hbm,
    off_hbm,
    level_hbm,
    rate_hbm,
    row_hbm,
    col_hbm,
    grad_ref,
    off_s,
    level_s,
    rate_s,
    off_v,
    level_v,
    row_taps,
    col_taps,
    dwell_x,
    pack_l,
    pack_r,
    recv_l,
    recv_r,
    corners,
    t_own,
    t_top,
    t_bot,
    wide,
    taps8,
    row_fwd,
    col_mat,
    row_adj,
    count,
    t_sum,
    along,
    back,
    send_sem,
    recv_sem,
    load_sem,
):
    sp = lax.axis_index("space")
    sc = lax.axis_index("scen")
    up, down, left, right = sp - 1, sp + 1, sc - 1, sc + 1
    has_up, has_down = sp > 0, sp < n_space - 1
    has_left, has_right = sc > 0, sc < n_scen - 1
    core = sp % 2
    other = (sc + n_scen // 2) % n_scen
    up_sc = jnp.where(core == 0, other, sc)
    down_sc = jnp.where(core == 0, sc, other)

    def first_tile(c):
        return jnp.minimum(jnp.maximum(c - 1, 0), n_scen - 3)

    def window(c):
        return pl.ds(pl.multiple_of(first_tile(c) * COLS, COLS), 3 * COLS)

    peers = (
        (up, sc, has_up),
        (down, sc, has_down),
        (sp, left, has_left),
        (sp, right, has_right),
        (up, left, has_up & has_left),
        (up, right, has_up & has_right),
        (down, left, has_down & has_left),
        (down, right, has_down & has_right),
        (up, up_sc, has_up),
        (down, down_sc, has_down),
    )
    comes = [peers[k][2] for k in (1, 0, 3, 2, 7, 6, 5, 4, 9, 8)]
    barrier = pltpu.get_barrier_semaphore()
    for row, col, there in peers:

        @pl.when(there)
        def _(row=row, col=col):
            pl.semaphore_signal(barrier, inc=1, device_id=(row, col), device_id_type=MESH)

    greeted = sum(jnp.where(there, 1, 0) for _, _, there in peers)

    load_dwell = pltpu.make_async_copy(
        dwell_hbm, dwell_x.at[RIM : RIM + ROWS, 0:COLS], load_sem.at[0]
    )
    load_target = pltpu.make_async_copy(target_hbm.at[:, window(sc)], t_own, load_sem.at[1])
    load_dwell.start()
    small = [
        pltpu.make_async_copy(src, dst, load_sem.at[2 + k])
        for k, (src, dst) in enumerate(
            (
                (row_hbm, row_taps),
                (col_hbm, col_taps),
                (rate_hbm, rate_s),
                (off_hbm, off_v),
                (level_hbm, level_v),
                (off_hbm, off_s),
                (level_hbm, level_s),
            )
        )
    ]
    for load in small:
        load.start()
    load_target.start()
    load_dwell.wait()

    low = lanes((1, COLS)) < RIM
    for g in range(4):
        base = RIM + 64 * g
        first = dwell_x[base : base + 32, 0:COLS].astype(F32)
        second = pltpu.roll(dwell_x[base + 32 : base + 64, 0:COLS].astype(F32), RIM, 1)
        pack_l[32 * g : 32 * g + 32, :] = jnp.where(low, first, second).astype(BF16)
        pack_r[32 * g : 32 * g + 32, :] = jnp.where(low, second, first).astype(BF16)

    pl.semaphore_wait(barrier, greeted)

    first_rows, last_rows = slice(0, RIM), slice(ROWS - RIM, ROWS)
    pairs = (
        (dwell_hbm.at[first_rows], dwell_x.at[RIM + ROWS : RIM + ROWS + RIM, 0:COLS]),
        (dwell_hbm.at[last_rows], dwell_x.at[0:RIM, 0:COLS]),
        (pack_l, recv_r),
        (pack_r, recv_l),
        (dwell_hbm.at[first_rows], corners.at[3]),
        (dwell_hbm.at[first_rows], corners.at[2]),
        (dwell_hbm.at[last_rows], corners.at[1]),
        (dwell_hbm.at[last_rows], corners.at[0]),
        (target_hbm.at[first_rows, window(up_sc)], t_bot),
        (target_hbm.at[last_rows, window(down_sc)], t_top),
    )
    copies = [
        pltpu.make_async_remote_copy(
            src_ref=src,
            dst_ref=dst,
            send_sem=send_sem.at[k],
            recv_sem=recv_sem.at[k],
            device_id=peers[k][:2],
            device_id_type=MESH,
        )
        for k, (src, dst) in enumerate(pairs)
    ]
    for k in (4, 5, 6, 7, 0, 1, 2, 3, 8, 9):
        pl.when(peers[k][2])(copies[k].start)

    def arrive(ks):
        for k in ks:
            pl.when(comes[k])(copies[k].wait_recv)

    side_ok = jnp.where(lanes((1, COLS)) < RIM, jnp.where(has_right, 1, 0), jnp.where(has_left, 1, 0)) > 0
    low = lanes((1, COLS)) < RIM

    for load in small:
        load.wait()

    taps8[...] = jnp.zeros_like(taps8)
    taps8[0:NRATE, 0:TAPS] = row_taps[...].astype(F32)
    taps8[4 : 4 + NRATE, 0:TAPS] = col_taps[...].astype(F32)
    taps = taps8[...]
    flip = jnp.where(
        lax.broadcasted_iota(jnp.int32, (RING, RING), 0) + lanes((RING, RING)) == TAPS - 1, 1.0, 0.0
    ).astype(BF16)
    reversed_taps = jnp.dot(taps.astype(BF16), flip, preferred_element_type=F32)

    def toeplitz(line, count_, first):
        return pltpu.roll(
            jnp.broadcast_to(line, (count_, RING)), first % RING, 1, stride=1, stride_axis=0
        ).astype(BF16)

    for q in range(NRATE):
        row_fwd[0, 160 * q : 160 * q + 160, :] = toeplitz(taps[q : q + 1], 160, 1)
        row_fwd[1, 160 * q : 160 * q + 160, :] = toeplitz(taps[q : q + 1], 160, 33)
        col_mat[q] = toeplitz(taps[4 + q : 5 + q], RING, -RADIUS)
        row_adj[:, RING * q : RING * q + RING] = toeplitz(reversed_taps[q : q + 1], 128, 1)

    offs = off_v[...]
    row_at = sp * ROWS + lax.broadcasted_iota(jnp.int32, (OUT, SCEN), 0) - 32 + offs[0:1, :]
    row_in = jnp.where((row_at >= 0) & (row_at < n_space * ROWS), 1.0, 0.0).astype(BF16)
    ring_at = lax.broadcasted_iota(jnp.int32, (RING, SCEN), 0)
    col_at = jnp.where(ring_at < COLS + RIM, ring_at, ring_at - RING) + sc * COLS + offs[1:2, :]
    col_in = jnp.where((col_at >= 0) & (col_at < n_scen * COLS), 1.0, 0.0)
    levels = level_v[...]
    for q in range(NRATE):
        mine = jnp.where(levels == q, 1.0, 0.0)
        seen = lax.dot_general(
            row_in, (col_in * mine).astype(BF16), (((1,), (1,)), ((), ())), preferred_element_type=F32
        )
        rate = rate_s[q]
        count[q] = seen * (rate * rate * (1.0 / SCEN))

    at = sc - first_tile(sc)

    def to_ring(ref, rows):
        own = ref[rows, pl.ds(pl.multiple_of(at * COLS, COLS), COLS)].astype(F32)
        after = ref[rows, pl.ds(pl.multiple_of(jnp.minimum(at + 1, 2) * COLS, COLS), COLS)].astype(F32)
        before = ref[rows, pl.ds(pl.multiple_of(jnp.maximum(at - 1, 0) * COLS, COLS), COLS)].astype(F32)
        return own, jnp.where(side_ok, jnp.where(low, after, before), 0.0)

    load_target.wait()
    own, side = to_ring(t_own, slice(0, ROWS))
    wide[0, RIM : RIM + ROWS, :] = own
    wide[1, RIM : RIM + ROWS, :] = side

    shift_rows = [off_s[0, s] for s in range(SCEN)]
    shift_cols = [lax.rem(RING - off_s[1, s], RING) for s in range(SCEN)]
    weights = [
        [jnp.where(level_s[0, s] == q, rate_s[q] * (1.0 / SCEN), 0.0) for q in range(NRATE)]
        for s in range(SCEN)
    ]

    def target_rows(c, carry):
        begin = c * CHUNK
        sums = [jnp.zeros((CHUNK, RING), F32) for _ in range(NRATE)]
        for s in range(SCEN):
            start = begin + 32 + shift_rows[s]
            part = jnp.concatenate([wide[side_, pl.ds(start, CHUNK), :] for side_ in range(2)], axis=1)
            part = pltpu.roll(part, shift_cols[s], 1)
            sums = [acc + weights[s][q] * part for q, acc in enumerate(sums)]
        for q in range(NRATE):
            t_sum[q, pl.ds(pl.multiple_of(begin, CHUNK), CHUNK), :] = sums[q]
        return carry

    lax.fori_loop(64 // CHUNK, 256 // CHUNK, target_rows, 0)

    arrive((8, 9))
    own, side = to_ring(t_top, slice(0, RIM))
    wide[0, 0:RIM, :] = jnp.where(has_up, own, 0.0)
    wide[1, 0:RIM, :] = jnp.where(has_up, side, 0.0)
    own, side = to_ring(t_bot, slice(0, RIM))
    wide[0, RIM + ROWS :, :] = jnp.where(has_down, own, 0.0)
    wide[1, RIM + ROWS :, :] = jnp.where(has_down, side, 0.0)
    lax.fori_loop(0, 64 // CHUNK, target_rows, 0)
    lax.fori_loop(256 // CHUNK, OUT // CHUNK, target_rows, 0)

    arrive(range(8))

    def corner(before, after, there):
        x = jnp.where(low, corners[after].astype(F32), corners[before].astype(F32))
        return jnp.where(there, jnp.where(side_ok, x, 0.0), 0.0).astype(BF16)

    dwell_x[0:RIM, 0:COLS] = jnp.where(has_up, dwell_x[0:RIM, 0:COLS].astype(F32), 0.0).astype(BF16)
    dwell_x[RIM + ROWS :, 0:COLS] = jnp.where(has_down, dwell_x[RIM + ROWS :, 0:COLS].astype(F32), 0.0).astype(BF16)
    dwell_x[0:RIM, COLS:RING] = corner(0, 1, has_up)
    dwell_x[RIM + ROWS :, COLS:RING] = corner(2, 3, has_down)
    for g in range(4):
        after = recv_r[32 * g : 32 * g + 32, :].astype(F32)
        before = recv_l[32 * g : 32 * g + 32, :].astype(F32)
        first = jnp.where(side_ok, jnp.where(low, after, before), 0.0)
        second = jnp.where(side_ok, pltpu.roll(jnp.where(low, before, after), RIM, 1), 0.0)
        base = RIM + 64 * g
        dwell_x[base : base + 32, COLS:RING] = first.astype(BF16)
        dwell_x[base + 32 : base + 64, COLS:RING] = second.astype(BF16)

    for half in range(2):
        product = jnp.dot(
            row_fwd[half], dwell_x[128 * half : 128 * half + 256, :], preferred_element_type=F32
        ).astype(BF16)
        for q in range(NRATE):
            along[q, 160 * half : 160 * half + 160, :] = product[160 * q : 160 * q + 160]

    for q in range(NRATE):
        base = lax.dot_general(
            along[q], col_mat[q], (((1,), (1,)), ((), ())), preferred_element_type=F32
        )
        misfit = (count[q] * base - t_sum[q]).astype(BF16)
        product = jnp.dot(misfit, col_mat[q, :, 0:COLS], preferred_element_type=F32).astype(BF16)
        back[RING * q : RING * q + 256, 0:COLS] = product[0:256]
        back[RING * q : RING * q + 192, COLS:RING] = product[128:OUT]
        back[RING * q + 192 : RING * q + 256, COLS:RING] = jnp.zeros((64, COLS), BF16)

    grad = jnp.dot(row_adj[...], back[...], preferred_element_type=F32)
    grad_ref[0:128, :] = grad[:, 0:COLS]
    grad_ref[128:256, :] = grad[:, COLS:RING]
    for k in range(10):
        pl.when(peers[k][2])(copies[k].wait_send)


def tile_step(n_space, n_scen, dwell, target, bound, offsets, level, rates, row_kernels, col_kernels):
    offsets, level = offsets.T, level.T
    vmem = pl.BlockSpec(memory_space=pltpu.VMEM)
    far = pl.BlockSpec(memory_space=pltpu.HBM)
    gradient = pl.pallas_call(
        functools.partial(kernel, n_space, n_scen),
        out_shape=jax.ShapeDtypeStruct((ROWS, COLS), F32),
        in_specs=[far] * 7,
        out_specs=vmem,
        scratch_shapes=[
            pltpu.SMEM((2, SCEN), jnp.int32),
            pltpu.SMEM((1, SCEN), jnp.int32),
            pltpu.SMEM((NRATE,), F32),
            pltpu.VMEM((2, SCEN), jnp.int32),
            pltpu.VMEM((1, SCEN), jnp.int32),
            pltpu.VMEM((NRATE, TAPS), BF16),
            pltpu.VMEM((NRATE, TAPS), BF16),
            pltpu.VMEM((384, RING), BF16),
            pltpu.VMEM((128, COLS), BF16),
            pltpu.VMEM((128, COLS), BF16),
            pltpu.VMEM((128, COLS), BF16),
            pltpu.VMEM((128, COLS), BF16),
            pltpu.VMEM((4, RIM, COLS), BF16),
            pltpu.VMEM((ROWS, 3 * COLS), BF16),
            pltpu.VMEM((RIM, 3 * COLS), BF16),
            pltpu.VMEM((RIM, 3 * COLS), BF16),
            pltpu.VMEM((2, 384, COLS), F32),
            pltpu.VMEM((8, RING), F32),
            pltpu.VMEM((2, NRATE * 160, RING), BF16),
            pltpu.VMEM((NRATE, RING, RING), BF16),
            pltpu.VMEM((128, NRATE * RING), BF16),
            pltpu.VMEM((NRATE, OUT, RING), F32),
            pltpu.VMEM((NRATE, OUT, RING), F32),
            pltpu.VMEM((NRATE, OUT, RING), BF16),
            pltpu.VMEM((NRATE * RING, RING), BF16),
            pltpu.SemaphoreType.DMA((10,)),
            pltpu.SemaphoreType.DMA((10,)),
            pltpu.SemaphoreType.DMA((9,)),
        ],
        compiler_params=pltpu.CompilerParams(collective_id=0, vmem_limit_bytes=63 * 1024 * 1024),
    )(dwell, target, offsets, level, rates, row_kernels, col_kernels)
    stepped = dwell.astype(F32) - STEP_SIZE * gradient
    return jnp.where(bound == 1, jnp.maximum(stepped, 0.0), stepped).astype(BF16)


def solution(mesh):
    return jax.shard_map(
        functools.partial(tile_step, mesh.shape["space"], mesh.shape["scen"]),
        mesh=mesh,
        in_specs=(P("space", "scen"), P("space", None), P("space", "scen"), P(), P(), P(), P(), P()),
        out_specs=P("space", "scen"),
        check_vma=False,
    )
```

```python
import functools

import jax
import jax.numpy as jnp
from jax import lax
from jax.experimental import pallas as pl
from jax.experimental.pallas import tpu as pltpu
from jax.sharding import PartitionSpec as P

MESH = pl.DeviceIdType.MESH
F32 = jnp.float32
BF16 = jnp.bfloat16

TAPS = 63
RADIUS = 31
ROWS = 256
COLS = 128
RIM = 64
RING = 256
OUT = 320
NRATE = 4
SCEN = 16
STEP_SIZE = 1.0


def lanes(shape):
    return lax.broadcasted_iota(jnp.int32, shape, len(shape) - 1)


def kernel(
    n_space,
    n_scen,
    dwell_hbm,
    target_hbm,
    off_hbm,
    level_hbm,
    rate_hbm,
    row_hbm,
    col_hbm,
    bound_hbm,
    next_ref,
    bound_v,
    off_s,
    level_s,
    rate_s,
    off_v,
    level_v,
    row_taps,
    col_taps,
    dwell_x,
    recv_l,
    recv_r,
    corners,
    t_own,
    t_top,
    t_bot,
    wide,
    taps8,
    row_fwd,
    col_mat,
    row_adj,
    col_tall,
    row_tall,
    col_pair,
    t_back,
    t_grad,
    count,
    along,
    back,
    send_sem,
    recv_sem,
    load_sem,
):
    sp = lax.axis_index("space")
    sc = lax.axis_index("scen")
    up, down, left, right = sp - 1, sp + 1, sc - 1, sc + 1
    has_up, has_down = sp > 0, sp < n_space - 1
    has_left, has_right = sc > 0, sc < n_scen - 1
    core = sp % 2
    other = (sc + n_scen // 2) % n_scen
    up_sc = jnp.where(core == 0, other, sc)
    down_sc = jnp.where(core == 0, sc, other)

    def first_tile(c):
        return jnp.minimum(jnp.maximum(c - 1, 0), n_scen - 3)

    def window(c):
        return pl.ds(pl.multiple_of(first_tile(c) * COLS, COLS), 3 * COLS)

    peers = (
        (up, sc, has_up),
        (down, sc, has_down),
        (sp, left, has_left),
        (sp, right, has_right),
        (up, left, has_up & has_left),
        (up, right, has_up & has_right),
        (down, left, has_down & has_left),
        (down, right, has_down & has_right),
        (up, up_sc, has_up),
        (down, down_sc, has_down),
    )
    comes = [peers[k][2] for k in (1, 0, 3, 2, 7, 6, 5, 4, 9, 8)]
    barrier = pltpu.get_barrier_semaphore()
    for row, col, there in [peers[k] for k in (4, 5, 6, 7, 0, 1, 8, 9, 2, 3)]:

        @pl.when(there)
        def _(row=row, col=col):
            pl.semaphore_signal(barrier, inc=1, device_id=(row, col), device_id_type=MESH)

    greeted = sum(jnp.where(there, 1, 0) for _, _, there in peers)

    load_dwell = pltpu.make_async_copy(
        dwell_hbm, dwell_x.at[RIM : RIM + ROWS, 0:COLS], load_sem.at[0]
    )
    load_target = pltpu.make_async_copy(target_hbm.at[:, window(sc)], t_own, load_sem.at[1])
    load_dwell.start()
    load_bound = pltpu.make_async_copy(bound_hbm, bound_v, load_sem.at[9])
    load_bound.start()
    small = [
        pltpu.make_async_copy(src, dst, load_sem.at[2 + k])
        for k, (src, dst) in enumerate(
            (
                (row_hbm, row_taps),
                (col_hbm, col_taps),
                (rate_hbm, rate_s),
                (off_hbm, off_v),
                (level_hbm, level_v),
                (off_hbm, off_s),
                (level_hbm, level_s),
            )
        )
    ]
    for load in small:
        load.start()
    load_target.start()
    load_dwell.wait()
    pl.semaphore_wait(barrier, greeted)

    first_rows, last_rows = slice(0, RIM), slice(ROWS - RIM, ROWS)
    own_tile = dwell_x.at[RIM : RIM + ROWS, 0:COLS]
    own_first, own_last = dwell_x.at[RIM : 2 * RIM, 0:COLS], dwell_x.at[ROWS : ROWS + RIM, 0:COLS]
    pairs = (
        (own_first, dwell_x.at[RIM + ROWS : RIM + ROWS + RIM, 0:COLS]),
        (own_last, dwell_x.at[0:RIM, 0:COLS]),
        (own_tile, recv_r),
        (own_tile, recv_l),
        (own_first, corners.at[3]),
        (own_first, corners.at[2]),
        (own_last, corners.at[1]),
        (own_last, corners.at[0]),
        (target_hbm.at[first_rows, window(up_sc)], t_bot),
        (target_hbm.at[last_rows, window(down_sc)], t_top),
    )
    copies = [
        pltpu.make_async_remote_copy(
            src_ref=src,
            dst_ref=dst,
            send_sem=send_sem.at[k],
            recv_sem=recv_sem.at[k],
            device_id=peers[k][:2],
            device_id_type=MESH,
        )
        for k, (src, dst) in enumerate(pairs)
    ]
    for k in (4, 5, 6, 7, 8, 9, 0, 1, 2, 3):
        pl.when(peers[k][2])(copies[k].start)

    def arrive(ks):
        for k in ks:
            pl.when(comes[k])(copies[k].wait_recv)

    side_ok = jnp.where(lanes((1, COLS)) < RIM, jnp.where(has_right, 1, 0), jnp.where(has_left, 1, 0)) > 0
    low = lanes((1, COLS)) < RIM

    for load in small:
        load.wait()

    taps8[...] = jnp.zeros_like(taps8)
    taps8[0:NRATE, 0:TAPS] = row_taps[...].astype(F32)
    taps8[4 : 4 + NRATE, 0:TAPS] = col_taps[...].astype(F32)
    taps = taps8[...]
    flip = jnp.where(
        lax.broadcasted_iota(jnp.int32, (RING, RING), 0) + lanes((RING, RING)) == TAPS - 1, 1.0, 0.0
    ).astype(BF16)
    reversed_taps = jnp.dot(taps.astype(BF16), flip, preferred_element_type=F32)

    def toeplitz(line, count_, first):
        return pltpu.roll(
            jnp.broadcast_to(line, (count_, RING)), first % RING, 1, stride=1, stride_axis=0
        )

    for q in range(NRATE):
        band = toeplitz(taps[q : q + 1], 192, 1).astype(BF16)
        row_fwd[0, 160 * q : 160 * q + 160, :] = band[0:160]
        row_fwd[1, 160 * q : 160 * q + 160, :] = band[32:192]
        band = toeplitz(taps[4 + q : 5 + q], 320, -RADIUS - 32)
        col_tall[q] = band[:, 0:COLS]
        col_mat[q] = band[32 : 32 + RING].astype(BF16)
        band = toeplitz(reversed_taps[q : q + 1], 192, 1)
        row_tall[q, 0] = band[:, 0:COLS]
        row_tall[q, 1] = band[:, COLS:RING]
        row_adj[:, RING * q : RING * q + RING] = band[0:128].astype(BF16)

    offs = off_v[...]
    row_at = sp * ROWS + lax.broadcasted_iota(jnp.int32, (OUT, SCEN), 0) - 32 + offs[0:1, :]
    row_in = jnp.where((row_at >= 0) & (row_at < n_space * ROWS), 1.0, 0.0).astype(BF16)
    ring_at = lax.broadcasted_iota(jnp.int32, (RING, SCEN), 0)
    col_at = jnp.where(ring_at < COLS + RIM, ring_at, ring_at - RING) + sc * COLS + offs[1:2, :]
    col_in = jnp.where((col_at >= 0) & (col_at < n_scen * COLS), 1.0, 0.0)
    levels = level_v[...]
    for q in range(NRATE):
        mine = jnp.where(levels == q, 1.0, 0.0)
        seen = lax.dot_general(
            row_in, (col_in * mine).astype(BF16), (((1,), (1,)), ((), ())), preferred_element_type=F32
        )
        rate = rate_s[q]
        count[q] = seen * (rate * rate * (1.0 / SCEN))

    at = sc - first_tile(sc)

    def to_ring(ref):
        own = ref[:, pl.ds(pl.multiple_of(at * COLS, COLS), COLS)].astype(F32)
        after = ref[:, pl.ds(pl.multiple_of(jnp.minimum(at + 1, 2) * COLS, COLS), COLS)].astype(F32)
        before = ref[:, pl.ds(pl.multiple_of(jnp.maximum(at - 1, 0) * COLS, COLS), COLS)].astype(F32)
        return own, jnp.where(side_ok, jnp.where(low, after, before), 0.0)

    load_target.wait()
    own, side = to_ring(t_own)
    wide[RIM : RIM + ROWS, 0:COLS] = own.astype(BF16)
    wide[RIM : RIM + ROWS, COLS:RING] = side.astype(BF16)

    shift_rows = [off_s[0, s] for s in range(SCEN)]
    shift_cols = [off_s[1, s] for s in range(SCEN)]
    level_of = [level_s[0, s] for s in range(SCEN)]
    weights = [rate_s[level_of[s]] * (1.0 / SCEN) for s in range(SCEN)]

    for pair in range(SCEN // 2):
        bands = [
            col_tall[level_of[s], pl.ds(32 - shift_cols[s], RING), :].astype(BF16)
            for s in (2 * pair, 2 * pair + 1)
        ]
        both = jnp.concatenate(bands, axis=1)
        col_pair[pair] = both
        product = jnp.dot(wide[RIM : RIM + ROWS, :], both, preferred_element_type=F32)
        for k in range(2):
            s = 2 * pair + k
            part = (product[:, COLS * k : COLS * k + COLS] * weights[s]).astype(BF16)
            t_back[s, RIM:256, 0:COLS] = part[0:192]
            t_back[s, 0:192, COLS:RING] = part[64:256]

    arrive((8, 9))
    for ref, there, begin in ((t_top, has_up, 0), (t_bot, has_down, RIM + ROWS)):
        own, side = to_ring(ref)
        wide[begin : begin + RIM, 0:COLS] = jnp.where(there, own, 0.0).astype(BF16)
        wide[begin : begin + RIM, COLS:RING] = jnp.where(there, side, 0.0).astype(BF16)
    rims = jnp.concatenate([wide[0:RIM, :], wide[RIM + ROWS :, :]], axis=0)
    for pair in range(SCEN // 2):
        product = jnp.dot(rims, col_pair[pair], preferred_element_type=F32)
        for k in range(2):
            s = 2 * pair + k
            part = (product[:, COLS * k : COLS * k + COLS] * weights[s]).astype(BF16)
            t_back[s, 0:RIM, 0:COLS] = part[0:RIM]
            t_back[s, 192:256, COLS:RING] = part[RIM:]
    total = jnp.zeros((128, RING), F32)
    for s in range(SCEN):
        band = jnp.concatenate(
            [row_tall[level_of[s], half, pl.ds(32 + shift_rows[s], 128), :] for half in range(2)], axis=1
        ).astype(BF16)
        total = total + jnp.dot(band, t_back[s], preferred_element_type=F32)
    t_grad[...] = total

    arrive(range(8))

    def corner(before, after, there):
        x = jnp.where(low, corners[after].astype(F32), corners[before].astype(F32))
        return jnp.where(there, jnp.where(side_ok, x, 0.0), 0.0).astype(BF16)

    dwell_x[0:RIM, 0:COLS] = jnp.where(has_up, dwell_x[0:RIM, 0:COLS].astype(F32), 0.0).astype(BF16)
    dwell_x[RIM + ROWS :, 0:COLS] = jnp.where(has_down, dwell_x[RIM + ROWS :, 0:COLS].astype(F32), 0.0).astype(BF16)
    dwell_x[0:RIM, COLS:RING] = corner(0, 1, has_up)
    dwell_x[RIM + ROWS :, COLS:RING] = corner(2, 3, has_down)
    dwell_x[RIM : RIM + ROWS, COLS:RING] = jnp.where(
        side_ok, jnp.where(low, recv_r[...].astype(F32), recv_l[...].astype(F32)), 0.0
    ).astype(BF16)

    for half in range(2):
        product = jnp.dot(
            row_fwd[half], dwell_x[128 * half : 128 * half + 256, :], preferred_element_type=F32
        ).astype(BF16)
        for q in range(NRATE):
            along[q, 160 * half : 160 * half + 160, :] = product[160 * q : 160 * q + 160]

    for q in range(NRATE):
        base = lax.dot_general(
            along[q], col_mat[q], (((1,), (1,)), ((), ())), preferred_element_type=F32
        )
        misfit = (count[q] * base).astype(BF16)
        product = jnp.dot(misfit, col_mat[q, :, 0:COLS], preferred_element_type=F32).astype(BF16)
        back[RING * q : RING * q + 256, 0:COLS] = product[0:256]
        back[RING * q : RING * q + 192, COLS:RING] = product[128:OUT]
        back[RING * q + 192 : RING * q + 256, COLS:RING] = jnp.zeros((64, COLS), BF16)

    grad = jnp.dot(row_adj[...], back[...], preferred_element_type=F32) - t_grad[...]
    load_bound.wait()
    for half in range(2):
        rows = slice(128 * half, 128 * half + 128)
        dwell = dwell_x[RIM + 128 * half : RIM + 128 * half + 128, 0:COLS].astype(F32)
        stepped = dwell - STEP_SIZE * grad[:, COLS * half : COLS * half + COLS]
        kept = jnp.where(bound_v[rows, :] == 1, jnp.maximum(stepped, 0.0), stepped)
        next_ref[rows, :] = kept.astype(BF16)
    for k in range(10):
        pl.when(peers[k][2])(copies[k].wait_send)


def tile_step(n_space, n_scen, dwell, target, bound, offsets, level, rates, row_kernels, col_kernels):
    offsets, level = offsets.T, level.T
    vmem = pl.BlockSpec(memory_space=pltpu.VMEM)
    far = pl.BlockSpec(memory_space=pltpu.HBM)
    return pl.pallas_call(
        functools.partial(kernel, n_space, n_scen),
        out_shape=pltpu.VMEM((ROWS, COLS), BF16),
        in_specs=[far] * 8,
        out_specs=vmem,
        scratch_shapes=[
            pltpu.VMEM((ROWS, COLS), jnp.int32),
            pltpu.SMEM((2, SCEN), jnp.int32),
            pltpu.SMEM((1, SCEN), jnp.int32),
            pltpu.SMEM((NRATE,), F32),
            pltpu.VMEM((2, SCEN), jnp.int32),
            pltpu.VMEM((1, SCEN), jnp.int32),
            pltpu.VMEM((NRATE, TAPS), BF16),
            pltpu.VMEM((NRATE, TAPS), BF16),
            pltpu.VMEM((384, RING), BF16),
            pltpu.VMEM((ROWS, COLS), BF16),
            pltpu.VMEM((ROWS, COLS), BF16),
            pltpu.VMEM((4, RIM, COLS), BF16),
            pltpu.VMEM((ROWS, 3 * COLS), BF16),
            pltpu.VMEM((RIM, 3 * COLS), BF16),
            pltpu.VMEM((RIM, 3 * COLS), BF16),
            pltpu.VMEM((384, RING), BF16),
            pltpu.VMEM((8, RING), F32),
            pltpu.VMEM((2, NRATE * 160, RING), BF16),
            pltpu.VMEM((NRATE, RING, RING), BF16),
            pltpu.VMEM((128, NRATE * RING), BF16),
            pltpu.VMEM((NRATE, OUT, COLS), F32),
            pltpu.VMEM((NRATE, 2, 192, COLS), F32),
            pltpu.VMEM((SCEN // 2, RING, RING), BF16),
            pltpu.VMEM((SCEN, RING, RING), BF16),
            pltpu.VMEM((128, RING), F32),
            pltpu.VMEM((NRATE, OUT, RING), F32),
            pltpu.VMEM((NRATE, OUT, RING), BF16),
            pltpu.VMEM((NRATE * RING, RING), BF16),
            pltpu.SemaphoreType.DMA((10,)),
            pltpu.SemaphoreType.DMA((10,)),
            pltpu.SemaphoreType.DMA((10,)),
        ],
        compiler_params=pltpu.CompilerParams(collective_id=0, vmem_limit_bytes=48 * 1024 * 1024),
    )(*(pltpu.with_memory_space_constraint(x, pltpu.HBM) for x in (dwell, target, offsets, level, rates, row_kernels, col_kernels, bound)))


def solution(mesh):
    return jax.shard_map(
        functools.partial(tile_step, mesh.shape["space"], mesh.shape["scen"]),
        mesh=mesh,
        in_specs=(P("space", "scen"), P("space", None), P("space", "scen"), P(), P(), P(), P(), P()),
        out_specs=P("space", "scen"),
        check_vma=False,
    )
```

```python
import functools

import jax
import jax.numpy as jnp
from jax import lax
from jax.experimental import pallas as pl
from jax.experimental.pallas import tpu as pltpu
from jax.sharding import PartitionSpec as P

MESH = pl.DeviceIdType.MESH
F32 = jnp.float32
BF16 = jnp.bfloat16

TAPS = 63
RADIUS = 31
ROWS = 256
COLS = 128
RIM = 64
RING = 256
OUT = 320
NRATE = 4
SCEN = 16
STEP_SIZE = 1.0


def lanes(shape):
    return lax.broadcasted_iota(jnp.int32, shape, len(shape) - 1)


def kernel(
    n_space,
    n_scen,
    dwell_hbm,
    target_hbm,
    off_hbm,
    level_hbm,
    rate_hbm,
    row_hbm,
    col_hbm,
    bound_hbm,
    next_ref,
    bound_v,
    off_s,
    level_s,
    rate_s,
    off_v,
    level_v,
    row_taps,
    col_taps,
    dwell_x,
    tile,
    rim_up,
    rim_down,
    pack_l,
    pack_r,
    recv_l,
    recv_r,
    corners,
    t_own,
    t_top,
    t_bot,
    wide,
    taps8,
    row_fwd,
    col_mat,
    row_adj,
    col_tall,
    row_tall,
    col_pair,
    t_back,
    t_grad,
    count,
    rim_band,
    along,
    back,
    send_sem,
    recv_sem,
    load_sem,
):
    sp = lax.axis_index("space")
    sc = lax.axis_index("scen")
    up, down, left, right = sp - 1, sp + 1, sc - 1, sc + 1
    has_up, has_down = sp > 0, sp < n_space - 1
    has_left, has_right = sc > 0, sc < n_scen - 1
    core = sp % 2
    other = (sc + n_scen // 2) % n_scen
    up_sc = jnp.where(core == 0, other, sc)
    down_sc = jnp.where(core == 0, sc, other)

    def first_tile(c):
        return jnp.minimum(jnp.maximum(c - 1, 0), n_scen - 3)

    def window(c):
        return pl.ds(pl.multiple_of(first_tile(c) * COLS, COLS), 3 * COLS)

    peers = (
        (up, sc, has_up),
        (down, sc, has_down),
        (sp, left, has_left),
        (sp, right, has_right),
        (up, left, has_up & has_left),
        (up, right, has_up & has_right),
        (down, left, has_down & has_left),
        (down, right, has_down & has_right),
        (up, up_sc, has_up),
        (down, down_sc, has_down),
    )
    comes = [peers[k][2] for k in (1, 0, 3, 2, 7, 6, 5, 4, 9, 8)]
    barrier = pltpu.get_barrier_semaphore()
    for row, col, there in [peers[k] for k in (4, 5, 6, 7, 0, 1, 8, 9, 2, 3)]:

        @pl.when(there)
        def _(row=row, col=col):
            pl.semaphore_signal(barrier, inc=1, device_id=(row, col), device_id_type=MESH)

    greeted = sum(jnp.where(there, 1, 0) for _, _, there in peers)

    load_dwell = pltpu.make_async_copy(
        dwell_hbm, tile, load_sem.at[0]
    )
    load_target = pltpu.make_async_copy(target_hbm.at[:, window(sc)], t_own, load_sem.at[1])
    load_dwell.start()
    load_bound = pltpu.make_async_copy(bound_hbm, bound_v, load_sem.at[9])
    load_bound.start()
    small = [
        pltpu.make_async_copy(src, dst, load_sem.at[2 + k])
        for k, (src, dst) in enumerate(
            (
                (row_hbm, row_taps),
                (col_hbm, col_taps),
                (rate_hbm, rate_s),
                (off_hbm, off_v),
                (level_hbm, level_v),
                (off_hbm, off_s),
                (level_hbm, level_s),
            )
        )
    ]
    for load in small:
        load.start()
    load_target.start()
    load_dwell.wait()
    low = lanes((1, COLS)) < RIM
    upper = tile[0:128, :].astype(F32)
    lower = pltpu.roll(tile[128:256, :].astype(F32), RIM, 1)
    pack_l[...] = jnp.where(low, upper, lower).astype(BF16)
    pack_r[...] = jnp.where(low, lower, upper).astype(BF16)
    pl.semaphore_wait(barrier, greeted)

    first_rows, last_rows = slice(0, RIM), slice(ROWS - RIM, ROWS)
    own_first, own_last = tile.at[first_rows], tile.at[last_rows]
    pairs = (
        (own_first, rim_down),
        (own_last, rim_up),
        (pack_l, recv_r),
        (pack_r, recv_l),
        (own_first, corners.at[3]),
        (own_first, corners.at[2]),
        (own_last, corners.at[1]),
        (own_last, corners.at[0]),
        (target_hbm.at[first_rows, window(up_sc)], t_bot),
        (target_hbm.at[last_rows, window(down_sc)], t_top),
    )
    copies = [
        pltpu.make_async_remote_copy(
            src_ref=src,
            dst_ref=dst,
            send_sem=send_sem.at[k],
            recv_sem=recv_sem.at[k],
            device_id=peers[k][:2],
            device_id_type=MESH,
        )
        for k, (src, dst) in enumerate(pairs)
    ]
    for k in (4, 5, 6, 7, 8, 9, 0, 1, 2, 3):
        pl.when(peers[k][2])(copies[k].start)

    def arrive(ks):
        for k in ks:
            pl.when(comes[k])(copies[k].wait_recv)

    side_ok = jnp.where(lanes((1, COLS)) < RIM, jnp.where(has_right, 1, 0), jnp.where(has_left, 1, 0)) > 0
    low = lanes((1, COLS)) < RIM

    for load in small:
        load.wait()

    taps8[...] = jnp.zeros_like(taps8)
    taps8[0:NRATE, 0:TAPS] = row_taps[...].astype(F32)
    taps8[4 : 4 + NRATE, 0:TAPS] = col_taps[...].astype(F32)
    taps = taps8[...]
    flip = jnp.where(
        lax.broadcasted_iota(jnp.int32, (RING, RING), 0) + lanes((RING, RING)) == TAPS - 1, 1.0, 0.0
    ).astype(BF16)
    reversed_taps = jnp.dot(taps.astype(BF16), flip, preferred_element_type=F32)

    def toeplitz(line, count_, first):
        return pltpu.roll(
            jnp.broadcast_to(line, (count_, RING)), first % RING, 1, stride=1, stride_axis=0
        )

    for q in range(NRATE):
        band = toeplitz(taps[q : q + 1], 192, 1).astype(BF16)
        row_fwd[0, 160 * q : 160 * q + 160, :] = band[0:160]
        row_fwd[1, 160 * q : 160 * q + 160, :] = band[32:192]
        band = toeplitz(taps[4 + q : 5 + q], 320, -RADIUS - 32)
        col_tall[q] = band[:, 0:COLS]
        col_mat[q] = band[32 : 32 + RING].astype(BF16)
        band = toeplitz(reversed_taps[q : q + 1], 192, 1)
        row_tall[q, 0] = band[:, 0:COLS]
        row_tall[q, 1] = band[:, COLS:RING]
        row_adj[:, RING * q : RING * q + RING] = band[0:128].astype(BF16)

    offs = off_v[...]
    row_at = sp * ROWS + lax.broadcasted_iota(jnp.int32, (OUT, SCEN), 0) - 32 + offs[0:1, :]
    row_in = jnp.where((row_at >= 0) & (row_at < n_space * ROWS), 1.0, 0.0).astype(BF16)
    ring_at = lax.broadcasted_iota(jnp.int32, (RING, SCEN), 0)
    col_at = jnp.where(ring_at < COLS + RIM, ring_at, ring_at - RING) + sc * COLS + offs[1:2, :]
    col_in = jnp.where((col_at >= 0) & (col_at < n_scen * COLS), 1.0, 0.0)
    levels = level_v[...]
    for q in range(NRATE):
        mine = jnp.where(levels == q, 1.0, 0.0)
        seen = lax.dot_general(
            row_in, (col_in * mine).astype(BF16), (((1,), (1,)), ((), ())), preferred_element_type=F32
        )
        rate = rate_s[q]
        count[q] = seen * (rate * rate * (1.0 / SCEN))

    at = sc - first_tile(sc)

    def to_ring(ref):
        own = ref[:, pl.ds(pl.multiple_of(at * COLS, COLS), COLS)].astype(F32)
        after = ref[:, pl.ds(pl.multiple_of(jnp.minimum(at + 1, 2) * COLS, COLS), COLS)].astype(F32)
        before = ref[:, pl.ds(pl.multiple_of(jnp.maximum(at - 1, 0) * COLS, COLS), COLS)].astype(F32)
        return own, jnp.where(side_ok, jnp.where(low, after, before), 0.0)

    load_target.wait()
    own, side = to_ring(t_own)
    wide[RIM : RIM + ROWS, 0:COLS] = own.astype(BF16)
    wide[RIM : RIM + ROWS, COLS:RING] = side.astype(BF16)

    shift_rows = [off_s[0, s] for s in range(SCEN)]
    shift_cols = [off_s[1, s] for s in range(SCEN)]
    level_of = [level_s[0, s] for s in range(SCEN)]
    weights = [rate_s[level_of[s]] * (1.0 / SCEN) for s in range(SCEN)]

    for pair in range(SCEN // 2):
        bands = [
            col_tall[level_of[s], pl.ds(32 - shift_cols[s], RING), :].astype(BF16)
            for s in (2 * pair, 2 * pair + 1)
        ]
        both = jnp.concatenate(bands, axis=1)
        col_pair[pair] = both
        product = jnp.dot(wide[RIM : RIM + ROWS, :], both, preferred_element_type=F32)
        for k in range(2):
            s = 2 * pair + k
            part = (product[:, COLS * k : COLS * k + COLS] * weights[s]).astype(BF16)
            t_back[s, RIM:256, 0:COLS] = part[0:192]
            t_back[s, 0:192, COLS:RING] = part[64:256]
            t_back[s, 0:RIM, 0:COLS] = jnp.zeros((RIM, COLS), BF16)
            t_back[s, 192:256, COLS:RING] = jnp.zeros((RIM, COLS), BF16)
            first = row_tall[level_of[s], 0, pl.ds(32 + shift_rows[s], 128), :]
            second = row_tall[level_of[s], 1, pl.ds(32 + shift_rows[s], 128), :]
            term = jnp.dot(
                jnp.concatenate([first, second], axis=1).astype(BF16), t_back[s], preferred_element_type=F32
            )
            t_grad[...] = term if s == 0 else t_grad[...] + term
            lanes_ = slice(COLS * k, COLS * k + COLS)
            rim_band[pair, 0:64, lanes_] = jnp.where(low, first[0:64], 0.0).astype(BF16)
            rim_band[pair, 64:128, lanes_] = jnp.where(low, 0.0, second[64:128]).astype(BF16)

    dwell_x[RIM : RIM + ROWS, 0:COLS] = tile[...]
    arrive((8, 9))
    for ref, there, begin in ((t_top, has_up, 0), (t_bot, has_down, RIM + ROWS)):
        own, side = to_ring(ref)
        wide[begin : begin + RIM, 0:COLS] = jnp.where(there, own, 0.0).astype(BF16)
        wide[begin : begin + RIM, COLS:RING] = jnp.where(there, side, 0.0).astype(BF16)
    rims = jnp.concatenate([wide[0:RIM, :], wide[RIM + ROWS :, :]], axis=0)
    total = jnp.zeros((128, COLS), F32)
    for pair in range(SCEN // 2):
        product = jnp.dot(rims, col_pair[pair], preferred_element_type=F32)
        parts = [
            (product[:, COLS * k : COLS * k + COLS] * weights[2 * pair + k]).astype(BF16) for k in range(2)
        ]
        total = total + jnp.dot(rim_band[pair], jnp.concatenate(parts, axis=0), preferred_element_type=F32)
    t_grad[0:64, 0:COLS] += total[0:64]
    t_grad[64:128, COLS:RING] += total[64:128]

    arrive(range(8))

    def corner(before, after, there):
        x = jnp.where(low, corners[after].astype(F32), corners[before].astype(F32))
        return jnp.where(there, jnp.where(side_ok, x, 0.0), 0.0).astype(BF16)

    dwell_x[0:RIM, 0:COLS] = jnp.where(has_up, rim_up[...].astype(F32), 0.0).astype(BF16)
    dwell_x[RIM + ROWS :, 0:COLS] = jnp.where(has_down, rim_down[...].astype(F32), 0.0).astype(BF16)
    dwell_x[0:RIM, COLS:RING] = corner(0, 1, has_up)
    dwell_x[RIM + ROWS :, COLS:RING] = corner(2, 3, has_down)
    after, before = recv_r[...].astype(F32), recv_l[...].astype(F32)
    upper = jnp.where(low, after, before)
    lower = pltpu.roll(jnp.where(low, before, after), RIM, 1)
    dwell_x[RIM : RIM + 128, COLS:RING] = jnp.where(side_ok, upper, 0.0).astype(BF16)
    dwell_x[RIM + 128 : RIM + ROWS, COLS:RING] = jnp.where(side_ok, lower, 0.0).astype(BF16)

    for half in range(2):
        product = jnp.dot(
            row_fwd[half], dwell_x[128 * half : 128 * half + 256, :], preferred_element_type=F32
        ).astype(BF16)
        for q in range(NRATE):
            along[q, 160 * half : 160 * half + 160, :] = product[160 * q : 160 * q + 160]

    for q in range(NRATE):
        base = lax.dot_general(
            along[q], col_mat[q], (((1,), (1,)), ((), ())), preferred_element_type=F32
        )
        misfit = (count[q] * base).astype(BF16)
        product = jnp.dot(misfit, col_mat[q, :, 0:COLS], preferred_element_type=F32).astype(BF16)
        back[RING * q : RING * q + 256, 0:COLS] = product[0:256]
        back[RING * q : RING * q + 192, COLS:RING] = product[128:OUT]
        back[RING * q + 192 : RING * q + 256, COLS:RING] = jnp.zeros((64, COLS), BF16)

    grad = jnp.dot(row_adj[...], back[...], preferred_element_type=F32) - t_grad[...]
    load_bound.wait()
    for half in range(2):
        rows = slice(128 * half, 128 * half + 128)
        dwell = dwell_x[RIM + 128 * half : RIM + 128 * half + 128, 0:COLS].astype(F32)
        stepped = dwell - STEP_SIZE * grad[:, COLS * half : COLS * half + COLS]
        kept = jnp.where(bound_v[rows, :] == 1, jnp.maximum(stepped, 0.0), stepped)
        next_ref[rows, :] = kept.astype(BF16)
    for k in range(10):
        pl.when(peers[k][2])(copies[k].wait_send)


def tile_step(n_space, n_scen, dwell, target, bound, offsets, level, rates, row_kernels, col_kernels):
    offsets, level = offsets.T, level.T
    vmem = pl.BlockSpec(memory_space=pltpu.VMEM)
    far = pl.BlockSpec(memory_space=pltpu.HBM)
    return pl.pallas_call(
        functools.partial(kernel, n_space, n_scen),
        out_shape=pltpu.VMEM((ROWS, COLS), BF16),
        in_specs=[far] * 8,
        out_specs=vmem,
        scratch_shapes=[
            pltpu.VMEM((ROWS, COLS), jnp.int32),
            pltpu.SMEM((2, SCEN), jnp.int32),
            pltpu.SMEM((1, SCEN), jnp.int32),
            pltpu.SMEM((NRATE,), F32),
            pltpu.VMEM((2, SCEN), jnp.int32),
            pltpu.VMEM((1, SCEN), jnp.int32),
            pltpu.VMEM((NRATE, TAPS), BF16),
            pltpu.VMEM((NRATE, TAPS), BF16),
            pltpu.VMEM((384, RING), BF16),
            pltpu.VMEM((ROWS, COLS), BF16),
            pltpu.VMEM((RIM, COLS), BF16),
            pltpu.VMEM((RIM, COLS), BF16),
            pltpu.VMEM((128, COLS), BF16),
            pltpu.VMEM((128, COLS), BF16),
            pltpu.VMEM((128, COLS), BF16),
            pltpu.VMEM((128, COLS), BF16),
            pltpu.VMEM((4, RIM, COLS), BF16),
            pltpu.VMEM((ROWS, 3 * COLS), BF16),
            pltpu.VMEM((RIM, 3 * COLS), BF16),
            pltpu.VMEM((RIM, 3 * COLS), BF16),
            pltpu.VMEM((384, RING), BF16),
            pltpu.VMEM((8, RING), F32),
            pltpu.VMEM((2, NRATE * 160, RING), BF16),
            pltpu.VMEM((NRATE, RING, RING), BF16),
            pltpu.VMEM((128, NRATE * RING), BF16),
            pltpu.VMEM((NRATE, OUT, COLS), F32),
            pltpu.VMEM((NRATE, 2, 192, COLS), F32),
            pltpu.VMEM((SCEN // 2, RING, RING), BF16),
            pltpu.VMEM((SCEN, RING, RING), BF16),
            pltpu.VMEM((128, RING), F32),
            pltpu.VMEM((NRATE, OUT, RING), F32),
            pltpu.VMEM((SCEN // 2, 128, RING), BF16),
            pltpu.VMEM((NRATE, OUT, RING), BF16),
            pltpu.VMEM((NRATE * RING, RING), BF16),
            pltpu.SemaphoreType.DMA((10,)),
            pltpu.SemaphoreType.DMA((10,)),
            pltpu.SemaphoreType.DMA((10,)),
        ],
        compiler_params=pltpu.CompilerParams(collective_id=0, vmem_limit_bytes=48 * 1024 * 1024),
    )(*(pltpu.with_memory_space_constraint(x, pltpu.HBM) for x in (dwell, target, offsets, level, rates, row_kernels, col_kernels, bound)))


def solution(mesh):
    return jax.shard_map(
        functools.partial(tile_step, mesh.shape["space"], mesh.shape["scen"]),
        mesh=mesh,
        in_specs=(P("space", "scen"), P("space", None), P("space", "scen"), P(), P(), P(), P(), P()),
        out_specs=P("space", "scen"),
        check_vma=False,
    )
```

```python
import functools

import jax
import jax.numpy as jnp
from jax import lax
from jax.experimental import pallas as pl
from jax.experimental.pallas import tpu as pltpu
from jax.sharding import PartitionSpec as P

MESH = pl.DeviceIdType.MESH
F32 = jnp.float32
BF16 = jnp.bfloat16

TAPS = 63
RADIUS = 31
ROWS = 256
COLS = 128
RIM = 64
RING = 256
OUT = 320
NRATE = 4
SCEN = 16
STEP_SIZE = 1.0


def lanes(shape):
    return lax.broadcasted_iota(jnp.int32, shape, len(shape) - 1)


def kernel(
    n_space,
    n_scen,
    dwell_hbm,
    target_hbm,
    off_hbm,
    level_hbm,
    rate_hbm,
    row_hbm,
    col_hbm,
    bound_hbm,
    next_ref,
    bound_v,
    off_s,
    level_s,
    rate_s,
    off_v,
    level_v,
    row_taps,
    col_taps,
    dwell_x,
    tile,
    rim_up,
    rim_down,
    pack_l,
    pack_r,
    recv_l,
    recv_r,
    corners,
    t_own,
    t_raw,
    t_send,
    t_top,
    t_bot,
    wide,
    taps8,
    row_fwd,
    col_mat,
    row_adj,
    col_tall,
    row_tall,
    col_pair,
    t_back,
    t_grad,
    count,
    rim_band,
    along,
    back,
    send_sem,
    recv_sem,
    load_sem,
):
    sp = lax.axis_index("space")
    sc = lax.axis_index("scen")
    up, down, left, right = sp - 1, sp + 1, sc - 1, sc + 1
    has_up, has_down = sp > 0, sp < n_space - 1
    has_left, has_right = sc > 0, sc < n_scen - 1
    core = sp % 2
    other = (sc + n_scen // 2) % n_scen
    up_sc = jnp.where(core == 0, other, sc)
    down_sc = jnp.where(core == 0, sc, other)

    def first_tile(c):
        return jnp.minimum(jnp.maximum(c - 1, 0), n_scen - 3)

    def window(c):
        return pl.ds(pl.multiple_of(first_tile(c) * COLS, COLS), 3 * COLS)

    peers = (
        (up, sc, has_up),
        (down, sc, has_down),
        (sp, left, has_left),
        (sp, right, has_right),
        (up, left, has_up & has_left),
        (up, right, has_up & has_right),
        (down, left, has_down & has_left),
        (down, right, has_down & has_right),
        (up, up_sc, has_up),
        (down, down_sc, has_down),
    )
    comes = [peers[k][2] for k in (1, 0, 3, 2, 7, 6, 5, 4, 9, 8)]
    barrier = pltpu.get_barrier_semaphore()
    for row, col, there in [peers[k] for k in (4, 5, 6, 7, 0, 1, 8, 9, 2, 3)]:

        @pl.when(there)
        def _(row=row, col=col):
            pl.semaphore_signal(barrier, inc=1, device_id=(row, col), device_id_type=MESH)

    greeted = sum(jnp.where(there, 1, 0) for _, _, there in peers)

    load_dwell = pltpu.make_async_copy(
        dwell_hbm, tile, load_sem.at[0]
    )
    load_target = pltpu.make_async_copy(target_hbm.at[:, window(sc)], t_own, load_sem.at[1])
    load_rims = [
        pltpu.make_async_copy(
            target_hbm.at[slice(begin, begin + RIM), window(col)], t_raw.at[k], load_sem.at[10 + k]
        )
        for k, (begin, col) in enumerate(((0, up_sc), (ROWS - RIM, down_sc)))
    ]
    load_dwell.start()
    for load in load_rims:
        load.start()
    load_bound = pltpu.make_async_copy(bound_hbm, bound_v, load_sem.at[9])
    load_bound.start()
    small = [
        pltpu.make_async_copy(src, dst, load_sem.at[2 + k])
        for k, (src, dst) in enumerate(
            (
                (row_hbm, row_taps),
                (col_hbm, col_taps),
                (rate_hbm, rate_s),
                (off_hbm, off_v),
                (level_hbm, level_v),
                (off_hbm, off_s),
                (level_hbm, level_s),
            )
        )
    ]
    for load in small:
        load.start()
    load_target.start()
    load_dwell.wait()
    low = lanes((1, COLS)) < RIM

    def to_ring(ref, col):
        at = col - first_tile(col)

        def pick(k):
            return ref[:, pl.ds(pl.multiple_of(k * COLS, COLS), COLS)].astype(F32)

        after = jnp.where(col < n_scen - 1, pick(jnp.minimum(at + 1, 2)), 0.0)
        before = jnp.where(col > 0, pick(jnp.maximum(at - 1, 0)), 0.0)
        return pick(at), jnp.where(low, after, before)

    upper = tile[0:128, :].astype(F32)
    lower = pltpu.roll(tile[128:256, :].astype(F32), RIM, 1)
    pack_l[...] = jnp.where(low, upper, lower).astype(BF16)
    pack_r[...] = jnp.where(low, lower, upper).astype(BF16)
    for k, col in enumerate((up_sc, down_sc)):
        load_rims[k].wait()
        own, side = to_ring(t_raw.at[k], col)
        t_send[k, :, 0:COLS] = own.astype(BF16)
        t_send[k, :, COLS:RING] = side.astype(BF16)

    @pl.when(sp == 0)
    def _():
        t_top[...] = jnp.zeros_like(t_top)
        rim_up[...] = jnp.zeros_like(rim_up)

    @pl.when(sp == n_space - 1)
    def _():
        t_bot[...] = jnp.zeros_like(t_bot)
        rim_down[...] = jnp.zeros_like(rim_down)

    pl.semaphore_wait(barrier, greeted)

    first_rows, last_rows = slice(0, RIM), slice(ROWS - RIM, ROWS)
    own_first, own_last = tile.at[first_rows], tile.at[last_rows]
    pairs = (
        (own_first, rim_down),
        (own_last, rim_up),
        (pack_l, recv_r),
        (pack_r, recv_l),
        (own_first, corners.at[3]),
        (own_first, corners.at[2]),
        (own_last, corners.at[1]),
        (own_last, corners.at[0]),
        (t_send.at[0], t_bot),
        (t_send.at[1], t_top),
    )
    copies = [
        pltpu.make_async_remote_copy(
            src_ref=src,
            dst_ref=dst,
            send_sem=send_sem.at[k],
            recv_sem=recv_sem.at[k],
            device_id=peers[k][:2],
            device_id_type=MESH,
        )
        for k, (src, dst) in enumerate(pairs)
    ]
    for k in (8, 9, 4, 5, 6, 7, 0, 1, 2, 3):
        pl.when(peers[k][2])(copies[k].start)

    def arrive(ks):
        for k in ks:
            pl.when(comes[k])(copies[k].wait_recv)

    side_ok = jnp.where(lanes((1, COLS)) < RIM, jnp.where(has_right, 1, 0), jnp.where(has_left, 1, 0)) > 0
    low = lanes((1, COLS)) < RIM

    for load in small:
        load.wait()

    taps8[...] = jnp.zeros_like(taps8)
    taps8[0:NRATE, 0:TAPS] = row_taps[...].astype(F32)
    taps8[4 : 4 + NRATE, 0:TAPS] = col_taps[...].astype(F32)
    taps = taps8[...]
    flip = jnp.where(
        lax.broadcasted_iota(jnp.int32, (RING, RING), 0) + lanes((RING, RING)) == TAPS - 1, 1.0, 0.0
    ).astype(BF16)
    reversed_taps = jnp.dot(taps.astype(BF16), flip, preferred_element_type=F32)

    def toeplitz(line, count_, first):
        return pltpu.roll(
            jnp.broadcast_to(line, (count_, RING)), first % RING, 1, stride=1, stride_axis=0
        )

    for q in range(NRATE):
        band = toeplitz(taps[q : q + 1], 192, 1).astype(BF16)
        row_fwd[0, 160 * q : 160 * q + 160, :] = band[0:160]
        row_fwd[1, 160 * q : 160 * q + 160, :] = band[32:192]
        band = toeplitz(taps[4 + q : 5 + q], 320, -RADIUS - 32)
        col_tall[q] = band[:, 0:COLS]
        col_mat[q] = band[32 : 32 + RING].astype(BF16)
        band = toeplitz(reversed_taps[q : q + 1], 192, 1)
        row_tall[q, 0] = band[:, 0:COLS]
        row_tall[q, 1] = band[:, COLS:RING]
        row_adj[:, RING * q : RING * q + RING] = band[0:128].astype(BF16)

    offs = off_v[...]
    row_at = sp * ROWS + lax.broadcasted_iota(jnp.int32, (OUT, SCEN), 0) - 32 + offs[0:1, :]
    row_in = jnp.where((row_at >= 0) & (row_at < n_space * ROWS), 1.0, 0.0).astype(BF16)
    ring_at = lax.broadcasted_iota(jnp.int32, (RING, SCEN), 0)
    col_at = jnp.where(ring_at < COLS + RIM, ring_at, ring_at - RING) + sc * COLS + offs[1:2, :]
    col_in = jnp.where((col_at >= 0) & (col_at < n_scen * COLS), 1.0, 0.0)
    levels = level_v[...]
    for q in range(NRATE):
        mine = jnp.where(levels == q, 1.0, 0.0)
        seen = lax.dot_general(
            row_in, (col_in * mine).astype(BF16), (((1,), (1,)), ((), ())), preferred_element_type=F32
        )
        rate = rate_s[q]
        count[q] = seen * (rate * rate * (1.0 / SCEN))

    load_target.wait()
    own, side = to_ring(t_own, sc)
    wide[:, 0:COLS] = own.astype(BF16)
    wide[:, COLS:RING] = side.astype(BF16)

    shift_rows = [off_s[0, s] for s in range(SCEN)]
    shift_cols = [off_s[1, s] for s in range(SCEN)]
    level_of = [level_s[0, s] for s in range(SCEN)]
    weights = [rate_s[level_of[s]] * (1.0 / SCEN) for s in range(SCEN)]

    for pair in range(SCEN // 2):
        bands = [
            col_tall[level_of[s], pl.ds(32 - shift_cols[s], RING), :].astype(BF16)
            for s in (2 * pair, 2 * pair + 1)
        ]
        both = jnp.concatenate(bands, axis=1)
        col_pair[pair] = both
        product = jnp.dot(wide[...], both, preferred_element_type=F32)
        for k in range(2):
            s = 2 * pair + k
            part = (product[:, COLS * k : COLS * k + COLS] * weights[s]).astype(BF16)
            t_back[s, RIM:256, 0:COLS] = part[0:192]
            t_back[s, 0:192, COLS:RING] = part[64:256]
            t_back[s, 0:RIM, 0:COLS] = jnp.zeros((RIM, COLS), BF16)
            t_back[s, 192:256, COLS:RING] = jnp.zeros((RIM, COLS), BF16)
            first = row_tall[level_of[s], 0, pl.ds(32 + shift_rows[s], 128), :]
            second = row_tall[level_of[s], 1, pl.ds(32 + shift_rows[s], 128), :]
            term = jnp.dot(
                jnp.concatenate([first, second], axis=1).astype(BF16), t_back[s], preferred_element_type=F32
            )
            t_grad[...] = term if s == 0 else t_grad[...] + term
            lanes_ = slice(COLS * k, COLS * k + COLS)
            rim_band[pair, 0:64, lanes_] = jnp.where(low, first[0:64], 0.0).astype(BF16)
            rim_band[pair, 64:128, lanes_] = jnp.where(low, 0.0, second[64:128]).astype(BF16)

    dwell_x[RIM : RIM + ROWS, 0:COLS] = tile[...]
    arrive((8, 9))
    rims = jnp.concatenate([t_top[...], t_bot[...]], axis=0)
    total = jnp.zeros((128, COLS), F32)
    for pair in range(SCEN // 2):
        product = jnp.dot(rims, col_pair[pair], preferred_element_type=F32)
        parts = [
            (product[:, COLS * k : COLS * k + COLS] * weights[2 * pair + k]).astype(BF16) for k in range(2)
        ]
        total = total + jnp.dot(rim_band[pair], jnp.concatenate(parts, axis=0), preferred_element_type=F32)
    t_grad[0:64, 0:COLS] += total[0:64]
    t_grad[64:128, COLS:RING] += total[64:128]

    arrive((2, 3))
    after, before = recv_r[...].astype(F32), recv_l[...].astype(F32)
    upper = jnp.where(low, after, before)
    lower = pltpu.roll(jnp.where(low, before, after), RIM, 1)
    dwell_x[RIM : RIM + 128, COLS:RING] = jnp.where(side_ok, upper, 0.0).astype(BF16)
    dwell_x[RIM + 128 : RIM + ROWS, COLS:RING] = jnp.where(side_ok, lower, 0.0).astype(BF16)

    arrive((0, 1))
    dwell_x[0:RIM, 0:COLS] = rim_up[...]
    dwell_x[RIM + ROWS :, 0:COLS] = rim_down[...]

    arrive((4, 5, 6, 7))

    def corner(before, after, there):
        x = jnp.where(low, corners[after].astype(F32), corners[before].astype(F32))
        return jnp.where(there, jnp.where(side_ok, x, 0.0), 0.0).astype(BF16)

    dwell_x[0:RIM, COLS:RING] = corner(0, 1, has_up)
    dwell_x[RIM + ROWS :, COLS:RING] = corner(2, 3, has_down)

    for half in range(2):
        product = jnp.dot(
            row_fwd[half], dwell_x[128 * half : 128 * half + 256, :], preferred_element_type=F32
        ).astype(BF16)
        for q in range(NRATE):
            along[q, 160 * half : 160 * half + 160, :] = product[160 * q : 160 * q + 160]

    for q in range(NRATE):
        base = lax.dot_general(
            along[q], col_mat[q], (((1,), (1,)), ((), ())), preferred_element_type=F32
        )
        misfit = (count[q] * base).astype(BF16)
        product = jnp.dot(misfit, col_mat[q, :, 0:COLS], preferred_element_type=F32).astype(BF16)
        back[RING * q : RING * q + 256, 0:COLS] = product[0:256]
        back[RING * q : RING * q + 192, COLS:RING] = product[128:OUT]
        back[RING * q + 192 : RING * q + 256, COLS:RING] = jnp.zeros((64, COLS), BF16)

    grad = jnp.dot(row_adj[...], back[...], preferred_element_type=F32) - t_grad[...]
    load_bound.wait()
    for half in range(2):
        rows = slice(128 * half, 128 * half + 128)
        dwell = dwell_x[RIM + 128 * half : RIM + 128 * half + 128, 0:COLS].astype(F32)
        stepped = dwell - STEP_SIZE * grad[:, COLS * half : COLS * half + COLS]
        kept = jnp.where(bound_v[rows, :] == 1, jnp.maximum(stepped, 0.0), stepped)
        next_ref[rows, :] = kept.astype(BF16)
    for k in range(10):
        pl.when(peers[k][2])(copies[k].wait_send)


def tile_step(n_space, n_scen, dwell, target, bound, offsets, level, rates, row_kernels, col_kernels):
    offsets, level = offsets.T, level.T
    vmem = pl.BlockSpec(memory_space=pltpu.VMEM)
    far = pl.BlockSpec(memory_space=pltpu.HBM)
    return pl.pallas_call(
        functools.partial(kernel, n_space, n_scen),
        out_shape=pltpu.VMEM((ROWS, COLS), BF16),
        in_specs=[far] * 8,
        out_specs=vmem,
        scratch_shapes=[
            pltpu.VMEM((ROWS, COLS), jnp.int32),
            pltpu.SMEM((2, SCEN), jnp.int32),
            pltpu.SMEM((1, SCEN), jnp.int32),
            pltpu.SMEM((NRATE,), F32),
            pltpu.VMEM((2, SCEN), jnp.int32),
            pltpu.VMEM((1, SCEN), jnp.int32),
            pltpu.VMEM((NRATE, TAPS), BF16),
            pltpu.VMEM((NRATE, TAPS), BF16),
            pltpu.VMEM((384, RING), BF16),
            pltpu.VMEM((ROWS, COLS), BF16),
            pltpu.VMEM((RIM, COLS), BF16),
            pltpu.VMEM((RIM, COLS), BF16),
            pltpu.VMEM((128, COLS), BF16),
            pltpu.VMEM((128, COLS), BF16),
            pltpu.VMEM((128, COLS), BF16),
            pltpu.VMEM((128, COLS), BF16),
            pltpu.VMEM((4, RIM, COLS), BF16),
            pltpu.VMEM((ROWS, 3 * COLS), BF16),
            pltpu.VMEM((2, RIM, 3 * COLS), BF16),
            pltpu.VMEM((2, RIM, RING), BF16),
            pltpu.VMEM((RIM, RING), BF16),
            pltpu.VMEM((RIM, RING), BF16),
            pltpu.VMEM((ROWS, RING), BF16),
            pltpu.VMEM((8, RING), F32),
            pltpu.VMEM((2, NRATE * 160, RING), BF16),
            pltpu.VMEM((NRATE, RING, RING), BF16),
            pltpu.VMEM((128, NRATE * RING), BF16),
            pltpu.VMEM((NRATE, OUT, COLS), F32),
            pltpu.VMEM((NRATE, 2, 192, COLS), F32),
            pltpu.VMEM((SCEN // 2, RING, RING), BF16),
            pltpu.VMEM((SCEN, RING, RING), BF16),
            pltpu.VMEM((128, RING), F32),
            pltpu.VMEM((NRATE, OUT, RING), F32),
            pltpu.VMEM((SCEN // 2, 128, RING), BF16),
            pltpu.VMEM((NRATE, OUT, RING), BF16),
            pltpu.VMEM((NRATE * RING, RING), BF16),
            pltpu.SemaphoreType.DMA((10,)),
            pltpu.SemaphoreType.DMA((10,)),
            pltpu.SemaphoreType.DMA((12,)),
        ],
        compiler_params=pltpu.CompilerParams(collective_id=0, vmem_limit_bytes=48 * 1024 * 1024),
    )(*(pltpu.with_memory_space_constraint(x, pltpu.HBM) for x in (dwell, target, offsets, level, rates, row_kernels, col_kernels, bound)))


def solution(mesh):
    return jax.shard_map(
        functools.partial(tile_step, mesh.shape["space"], mesh.shape["scen"]),
        mesh=mesh,
        in_specs=(P("space", "scen"), P("space", None), P("space", "scen"), P(), P(), P(), P(), P()),
        out_specs=P("space", "scen"),
        check_vma=False,
    )
```

```python
import functools

import jax
import jax.numpy as jnp
from jax import lax
from jax.experimental import pallas as pl
from jax.experimental.pallas import tpu as pltpu
from jax.sharding import PartitionSpec as P

MESH = pl.DeviceIdType.MESH
F32 = jnp.float32
BF16 = jnp.bfloat16

TAPS = 63
RADIUS = 31
ROWS = 256
COLS = 128
RIM = 64
RING = 256
OUT = 320
NRATE = 4
SCEN = 16
STEP_SIZE = 1.0


def lanes(shape):
    return lax.broadcasted_iota(jnp.int32, shape, len(shape) - 1)


def kernel(
    n_space,
    n_scen,
    dwell_hbm,
    target_hbm,
    off_hbm,
    level_hbm,
    rate_hbm,
    row_hbm,
    col_hbm,
    bound_hbm,
    next_ref,
    bound_v,
    off_s,
    level_s,
    rate_s,
    off_v,
    level_v,
    row_taps,
    col_taps,
    dwell_x,
    tile,
    rim_up,
    rim_down,
    pack_l,
    pack_r,
    recv_l,
    recv_r,
    corners,
    t_own,
    t_raw,
    t_send,
    t_top,
    t_bot,
    wide,
    taps8,
    row_fwd,
    col_mat,
    row_adj,
    col_tall,
    row_tall,
    col_pair,
    t_back,
    t_grad,
    count,
    rim_band,
    along,
    back,
    send_sem,
    recv_sem,
    load_sem,
):
    sp = lax.axis_index("space")
    sc = lax.axis_index("scen")
    up, down, left, right = sp - 1, sp + 1, sc - 1, sc + 1
    has_up, has_down = sp > 0, sp < n_space - 1
    has_left, has_right = sc > 0, sc < n_scen - 1
    core = sp % 2
    other = (sc + n_scen // 2) % n_scen
    up_sc = jnp.where(core == 0, other, sc)
    down_sc = jnp.where(core == 0, sc, other)

    def first_tile(c):
        return jnp.minimum(jnp.maximum(c - 1, 0), n_scen - 3)

    def window(c):
        return pl.ds(pl.multiple_of(first_tile(c) * COLS, COLS), 3 * COLS)

    peers = (
        (up, sc, has_up),
        (down, sc, has_down),
        (sp, left, has_left),
        (sp, right, has_right),
        (up, left, has_up & has_left),
        (up, right, has_up & has_right),
        (down, left, has_down & has_left),
        (down, right, has_down & has_right),
        (up, up_sc, has_up),
        (down, down_sc, has_down),
    )
    comes = [peers[k][2] for k in (1, 0, 3, 2, 7, 6, 5, 4, 9, 8)]
    barrier = pltpu.get_barrier_semaphore()
    for row, col, there in [peers[k] for k in (4, 5, 6, 7, 0, 1, 8, 9, 2, 3)]:

        @pl.when(there)
        def _(row=row, col=col):
            pl.semaphore_signal(barrier, inc=1, device_id=(row, col), device_id_type=MESH)

    greeted = sum(jnp.where(there, 1, 0) for _, _, there in peers)

    load_dwell = pltpu.make_async_copy(
        dwell_hbm, tile, load_sem.at[0]
    )
    load_target = pltpu.make_async_copy(target_hbm.at[:, window(sc)], t_own, load_sem.at[1])
    load_rims = [
        pltpu.make_async_copy(
            target_hbm.at[slice(begin, begin + RIM), window(col)], t_raw.at[k], load_sem.at[10 + k]
        )
        for k, (begin, col) in enumerate(((0, up_sc), (ROWS - RIM, down_sc)))
    ]
    load_dwell.start()
    for load in load_rims:
        load.start()
    load_bound = pltpu.make_async_copy(bound_hbm, bound_v, load_sem.at[9])
    load_bound.start()
    small = [
        pltpu.make_async_copy(src, dst, load_sem.at[2 + k])
        for k, (src, dst) in enumerate(
            (
                (row_hbm, row_taps),
                (col_hbm, col_taps),
                (rate_hbm, rate_s),
                (off_hbm, off_v),
                (level_hbm, level_v),
                (off_hbm, off_s),
                (level_hbm, level_s),
            )
        )
    ]
    for load in small:
        load.start()
    load_target.start()
    load_dwell.wait()
    low = lanes((1, COLS)) < RIM

    def to_ring(ref, col):
        at = col - first_tile(col)

        def pick(k):
            return ref[:, pl.ds(pl.multiple_of(k * COLS, COLS), COLS)].astype(F32)

        after = jnp.where(col < n_scen - 1, pick(jnp.minimum(at + 1, 2)), 0.0)
        before = jnp.where(col > 0, pick(jnp.maximum(at - 1, 0)), 0.0)
        return pick(at), jnp.where(low, after, before)

    for g in range(4):
        upper = tile[64 * g : 64 * g + 32, :].astype(F32)
        lower = pltpu.roll(tile[64 * g + 32 : 64 * g + 64, :].astype(F32), RIM, 1)
        pack_l[32 * g : 32 * g + 32, :] = jnp.where(low, upper, lower).astype(BF16)
        pack_r[32 * g : 32 * g + 32, :] = jnp.where(low, lower, upper).astype(BF16)
    for k, col in enumerate((up_sc, down_sc)):
        load_rims[k].wait()
        own, side = to_ring(t_raw.at[k], col)
        t_send[k, :, 0:COLS] = own.astype(BF16)
        t_send[k, :, COLS:RING] = side.astype(BF16)

    @pl.when(sp == 0)
    def _():
        t_top[...] = jnp.zeros_like(t_top)
        rim_up[...] = jnp.zeros_like(rim_up)

    @pl.when(sp == n_space - 1)
    def _():
        t_bot[...] = jnp.zeros_like(t_bot)
        rim_down[...] = jnp.zeros_like(rim_down)

    pl.semaphore_wait(barrier, greeted)

    first_rows, last_rows = slice(0, RIM), slice(ROWS - RIM, ROWS)
    own_first, own_last = tile.at[first_rows], tile.at[last_rows]
    pairs = (
        (own_first, rim_down),
        (own_last, rim_up),
        (pack_l, recv_r),
        (pack_r, recv_l),
        (pack_l.at[0:32], corners.at[3]),
        (pack_r.at[0:32], corners.at[2]),
        (pack_l.at[96:128], corners.at[1]),
        (pack_r.at[96:128], corners.at[0]),
        (t_send.at[0], t_bot),
        (t_send.at[1], t_top),
    )
    copies = [
        pltpu.make_async_remote_copy(
            src_ref=src,
            dst_ref=dst,
            send_sem=send_sem.at[k],
            recv_sem=recv_sem.at[k],
            device_id=peers[k][:2],
            device_id_type=MESH,
        )
        for k, (src, dst) in enumerate(pairs)
    ]
    for k in (8, 9, 4, 5, 6, 7, 2, 3, 0, 1):
        pl.when(peers[k][2])(copies[k].start)

    def arrive(ks):
        for k in ks:
            pl.when(comes[k])(copies[k].wait_recv)

    side_ok = jnp.where(lanes((1, COLS)) < RIM, jnp.where(has_right, 1, 0), jnp.where(has_left, 1, 0)) > 0
    low = lanes((1, COLS)) < RIM

    for load in small:
        load.wait()

    taps8[...] = jnp.zeros_like(taps8)
    taps8[0:NRATE, 0:TAPS] = row_taps[...].astype(F32)
    taps8[4 : 4 + NRATE, 0:TAPS] = col_taps[...].astype(F32)
    taps = taps8[...]
    flip = jnp.where(
        lax.broadcasted_iota(jnp.int32, (RING, RING), 0) + lanes((RING, RING)) == TAPS - 1, 1.0, 0.0
    ).astype(BF16)
    reversed_taps = jnp.dot(taps.astype(BF16), flip, preferred_element_type=F32)

    def toeplitz(line, count_, first):
        return pltpu.roll(
            jnp.broadcast_to(line, (count_, RING)), first % RING, 1, stride=1, stride_axis=0
        )

    for q in range(NRATE):
        band = toeplitz(taps[q : q + 1], 192, 1).astype(BF16)
        row_fwd[0, 160 * q : 160 * q + 160, :] = band[0:160]
        row_fwd[1, 160 * q : 160 * q + 160, :] = band[32:192]
        band = toeplitz(taps[4 + q : 5 + q], 320, -RADIUS - 32)
        col_tall[q] = band[:, 0:COLS]
        col_mat[q] = band[32 : 32 + RING].astype(BF16)
        band = toeplitz(reversed_taps[q : q + 1], 192, 1)
        row_tall[q, 0] = band[:, 0:COLS]
        row_tall[q, 1] = band[:, COLS:RING]
        row_adj[:, RING * q : RING * q + RING] = band[0:128].astype(BF16)

    offs = off_v[...]
    row_at = sp * ROWS + lax.broadcasted_iota(jnp.int32, (OUT, SCEN), 0) - 32 + offs[0:1, :]
    row_in = jnp.where((row_at >= 0) & (row_at < n_space * ROWS), 1.0, 0.0).astype(BF16)
    ring_at = lax.broadcasted_iota(jnp.int32, (RING, SCEN), 0)
    col_at = jnp.where(ring_at < COLS + RIM, ring_at, ring_at - RING) + sc * COLS + offs[1:2, :]
    col_in = jnp.where((col_at >= 0) & (col_at < n_scen * COLS), 1.0, 0.0)
    levels = level_v[...]
    for q in range(NRATE):
        mine = jnp.where(levels == q, 1.0, 0.0)
        seen = lax.dot_general(
            row_in, (col_in * mine).astype(BF16), (((1,), (1,)), ((), ())), preferred_element_type=F32
        )
        rate = rate_s[q]
        count[q] = seen * (rate * rate * (1.0 / SCEN))

    load_target.wait()
    own, side = to_ring(t_own, sc)
    wide[:, 0:COLS] = own.astype(BF16)
    wide[:, COLS:RING] = side.astype(BF16)

    shift_rows = [off_s[0, s] for s in range(SCEN)]
    shift_cols = [off_s[1, s] for s in range(SCEN)]
    level_of = [level_s[0, s] for s in range(SCEN)]
    weights = [rate_s[level_of[s]] * (1.0 / SCEN) for s in range(SCEN)]

    for pair in range(SCEN // 2):
        bands = [
            col_tall[level_of[s], pl.ds(32 - shift_cols[s], RING), :].astype(BF16)
            for s in (2 * pair, 2 * pair + 1)
        ]
        both = jnp.concatenate(bands, axis=1)
        col_pair[pair] = both
        product = jnp.dot(wide[...], both, preferred_element_type=F32)
        for k in range(2):
            s = 2 * pair + k
            part = (product[:, COLS * k : COLS * k + COLS] * weights[s]).astype(BF16)
            t_back[s, RIM:256, 0:COLS] = part[0:192]
            t_back[s, 0:192, COLS:RING] = part[64:256]
            t_back[s, 0:RIM, 0:COLS] = jnp.zeros((RIM, COLS), BF16)
            t_back[s, 192:256, COLS:RING] = jnp.zeros((RIM, COLS), BF16)
            first = row_tall[level_of[s], 0, pl.ds(32 + shift_rows[s], 128), :]
            second = row_tall[level_of[s], 1, pl.ds(32 + shift_rows[s], 128), :]
            term = jnp.dot(
                jnp.concatenate([first, second], axis=1).astype(BF16), t_back[s], preferred_element_type=F32
            )
            t_grad[...] = term if s == 0 else t_grad[...] + term
            lanes_ = slice(COLS * k, COLS * k + COLS)
            rim_band[pair, 0:64, lanes_] = jnp.where(low, first[0:64], 0.0).astype(BF16)
            rim_band[pair, 64:128, lanes_] = jnp.where(low, 0.0, second[64:128]).astype(BF16)

    dwell_x[RIM : RIM + ROWS, 0:COLS] = tile[...]
    arrive((8, 9))
    rims = jnp.concatenate([t_top[...], t_bot[...]], axis=0)
    total = jnp.zeros((128, COLS), F32)
    for pair in range(SCEN // 2):
        product = jnp.dot(rims, col_pair[pair], preferred_element_type=F32)
        parts = [
            (product[:, COLS * k : COLS * k + COLS] * weights[2 * pair + k]).astype(BF16) for k in range(2)
        ]
        total = total + jnp.dot(rim_band[pair], jnp.concatenate(parts, axis=0), preferred_element_type=F32)
    t_grad[0:64, 0:COLS] += total[0:64]
    t_grad[64:128, COLS:RING] += total[64:128]

    arrive((2, 3))
    def unpack(begin, after, before, there):
        after, before = after.astype(F32), before.astype(F32)
        upper = jnp.where(low, after, before)
        lower = pltpu.roll(jnp.where(low, before, after), RIM, 1)
        for half, x in enumerate((upper, lower)):
            kept = jnp.where(side_ok, x, 0.0)
            dwell_x[begin + 32 * half : begin + 32 * half + 32, COLS:RING] = jnp.where(there, kept, 0.0).astype(BF16)

    for g in range(4):
        rows = slice(32 * g, 32 * g + 32)
        unpack(RIM + 64 * g, recv_r[rows, :], recv_l[rows, :], True)

    arrive((0, 1))
    dwell_x[0:RIM, 0:COLS] = rim_up[...]
    dwell_x[RIM + ROWS :, 0:COLS] = rim_down[...]

    arrive((4, 5, 6, 7))

    unpack(0, corners[1], corners[0], has_up)
    unpack(RIM + ROWS, corners[3], corners[2], has_down)

    for half in range(2):
        product = jnp.dot(
            row_fwd[half], dwell_x[128 * half : 128 * half + 256, :], preferred_element_type=F32
        ).astype(BF16)
        for q in range(NRATE):
            along[q, 160 * half : 160 * half + 160, :] = product[160 * q : 160 * q + 160]

    for q in range(NRATE):
        base = lax.dot_general(
            along[q], col_mat[q], (((1,), (1,)), ((), ())), preferred_element_type=F32
        )
        misfit = (count[q] * base).astype(BF16)
        product = jnp.dot(misfit, col_mat[q, :, 0:COLS], preferred_element_type=F32).astype(BF16)
        back[RING * q : RING * q + 256, 0:COLS] = product[0:256]
        back[RING * q : RING * q + 192, COLS:RING] = product[128:OUT]
        back[RING * q + 192 : RING * q + 256, COLS:RING] = jnp.zeros((64, COLS), BF16)

    grad = jnp.dot(row_adj[...], back[...], preferred_element_type=F32) - t_grad[...]
    load_bound.wait()
    for half in range(2):
        rows = slice(128 * half, 128 * half + 128)
        dwell = dwell_x[RIM + 128 * half : RIM + 128 * half + 128, 0:COLS].astype(F32)
        stepped = dwell - STEP_SIZE * grad[:, COLS * half : COLS * half + COLS]
        kept = jnp.where(bound_v[rows, :] == 1, jnp.maximum(stepped, 0.0), stepped)
        next_ref[rows, :] = kept.astype(BF16)
    for k in range(10):
        pl.when(peers[k][2])(copies[k].wait_send)


def tile_step(n_space, n_scen, dwell, target, bound, offsets, level, rates, row_kernels, col_kernels):
    offsets, level = offsets.T, level.T
    vmem = pl.BlockSpec(memory_space=pltpu.VMEM)
    far = pl.BlockSpec(memory_space=pltpu.HBM)
    return pl.pallas_call(
        functools.partial(kernel, n_space, n_scen),
        out_shape=pltpu.VMEM((ROWS, COLS), BF16),
        in_specs=[far] * 8,
        out_specs=vmem,
        scratch_shapes=[
            pltpu.VMEM((ROWS, COLS), jnp.int32),
            pltpu.SMEM((2, SCEN), jnp.int32),
            pltpu.SMEM((1, SCEN), jnp.int32),
            pltpu.SMEM((NRATE,), F32),
            pltpu.VMEM((2, SCEN), jnp.int32),
            pltpu.VMEM((1, SCEN), jnp.int32),
            pltpu.VMEM((NRATE, TAPS), BF16),
            pltpu.VMEM((NRATE, TAPS), BF16),
            pltpu.VMEM((384, RING), BF16),
            pltpu.VMEM((ROWS, COLS), BF16),
            pltpu.VMEM((RIM, COLS), BF16),
            pltpu.VMEM((RIM, COLS), BF16),
            pltpu.VMEM((128, COLS), BF16),
            pltpu.VMEM((128, COLS), BF16),
            pltpu.VMEM((128, COLS), BF16),
            pltpu.VMEM((128, COLS), BF16),
            pltpu.VMEM((4, 32, COLS), BF16),
            pltpu.VMEM((ROWS, 3 * COLS), BF16),
            pltpu.VMEM((2, RIM, 3 * COLS), BF16),
            pltpu.VMEM((2, RIM, RING), BF16),
            pltpu.VMEM((RIM, RING), BF16),
            pltpu.VMEM((RIM, RING), BF16),
            pltpu.VMEM((ROWS, RING), BF16),
            pltpu.VMEM((8, RING), F32),
            pltpu.VMEM((2, NRATE * 160, RING), BF16),
            pltpu.VMEM((NRATE, RING, RING), BF16),
            pltpu.VMEM((128, NRATE * RING), BF16),
            pltpu.VMEM((NRATE, OUT, COLS), F32),
            pltpu.VMEM((NRATE, 2, 192, COLS), F32),
            pltpu.VMEM((SCEN // 2, RING, RING), BF16),
            pltpu.VMEM((SCEN, RING, RING), BF16),
            pltpu.VMEM((128, RING), F32),
            pltpu.VMEM((NRATE, OUT, RING), F32),
            pltpu.VMEM((SCEN // 2, 128, RING), BF16),
            pltpu.VMEM((NRATE, OUT, RING), BF16),
            pltpu.VMEM((NRATE * RING, RING), BF16),
            pltpu.SemaphoreType.DMA((10,)),
            pltpu.SemaphoreType.DMA((10,)),
            pltpu.SemaphoreType.DMA((12,)),
        ],
        compiler_params=pltpu.CompilerParams(collective_id=0, vmem_limit_bytes=48 * 1024 * 1024),
    )(*(pltpu.with_memory_space_constraint(x, pltpu.HBM) for x in (dwell, target, offsets, level, rates, row_kernels, col_kernels, bound)))


def solution(mesh):
    return jax.shard_map(
        functools.partial(tile_step, mesh.shape["space"], mesh.shape["scen"]),
        mesh=mesh,
        in_specs=(P("space", "scen"), P("space", None), P("space", "scen"), P(), P(), P(), P(), P()),
        out_specs=P("space", "scen"),
        check_vma=False,
    )
```

```python
import functools

import jax
import jax.numpy as jnp
from jax import lax
from jax.experimental import pallas as pl
from jax.experimental.pallas import tpu as pltpu
from jax.sharding import PartitionSpec as P

MESH = pl.DeviceIdType.MESH
F32 = jnp.float32
BF16 = jnp.bfloat16

TAPS = 63
RADIUS = 31
ROWS = 256
COLS = 128
RIM = 64
RING = 256
OUT = 320
NRATE = 4
SCEN = 16
STEP_SIZE = 1.0


def lanes(shape):
    return lax.broadcasted_iota(jnp.int32, shape, len(shape) - 1)


def kernel(
    n_space,
    n_scen,
    dwell_hbm,
    target_hbm,
    off_hbm,
    level_hbm,
    rate_hbm,
    row_hbm,
    col_hbm,
    bound_hbm,
    next_ref,
    bound_v,
    off_s,
    level_s,
    rate_s,
    off_v,
    level_v,
    row_taps,
    col_taps,
    dwell_x,
    tile,
    rim_up,
    rim_down,
    pack_l,
    pack_r,
    recv_l,
    recv_r,
    corners,
    t_own,
    t_raw,
    t_send,
    t_top,
    t_bot,
    wide,
    taps8,
    row_fwd,
    col_mat,
    row_adj,
    col_tall,
    row_tall,
    col_pair,
    t_back,
    t_grad,
    count,
    rim_band,
    along,
    back,
    send_sem,
    recv_sem,
    load_sem,
):
    sp = lax.axis_index("space")
    sc = lax.axis_index("scen")
    up, down, left, right = sp - 1, sp + 1, sc - 1, sc + 1
    has_up, has_down = sp > 0, sp < n_space - 1
    has_left, has_right = sc > 0, sc < n_scen - 1
    core = sp % 2
    other = (sc + n_scen // 2) % n_scen
    up_sc = jnp.where(core == 0, other, sc)
    down_sc = jnp.where(core == 0, sc, other)

    def first_tile(c):
        return jnp.minimum(jnp.maximum(c - 1, 0), n_scen - 3)

    def window(c):
        return pl.ds(pl.multiple_of(first_tile(c) * COLS, COLS), 3 * COLS)

    peers = (
        (up, sc, has_up),
        (down, sc, has_down),
        (sp, left, has_left),
        (sp, right, has_right),
        (up, left, has_up & has_left),
        (up, right, has_up & has_right),
        (down, left, has_down & has_left),
        (down, right, has_down & has_right),
        (up, up_sc, has_up),
        (down, down_sc, has_down),
    )
    comes = [peers[k][2] for k in (1, 0, 3, 2, 7, 6, 5, 4, 9, 8)]
    barrier = pltpu.get_barrier_semaphore()
    for row, col, there in [peers[k] for k in (4, 5, 6, 7, 0, 1, 8, 9, 2, 3)]:

        @pl.when(there)
        def _(row=row, col=col):
            pl.semaphore_signal(barrier, inc=1, device_id=(row, col), device_id_type=MESH)

    greeted = sum(jnp.where(there, 1, 0) for _, _, there in peers)

    load_dwell = pltpu.make_async_copy(
        dwell_hbm, tile, load_sem.at[0]
    )
    load_target = pltpu.make_async_copy(target_hbm.at[:, window(sc)], t_own, load_sem.at[1])
    load_rims = [
        pltpu.make_async_copy(
            target_hbm.at[slice(begin, begin + RIM), window(col)], t_raw.at[k], load_sem.at[10 + k]
        )
        for k, (begin, col) in enumerate(((0, up_sc), (ROWS - RIM, down_sc)))
    ]
    load_dwell.start()
    for load in load_rims:
        load.start()
    load_bound = pltpu.make_async_copy(bound_hbm, bound_v, load_sem.at[9])
    load_bound.start()
    small = [
        pltpu.make_async_copy(src, dst, load_sem.at[2 + k])
        for k, (src, dst) in enumerate(
            (
                (row_hbm, row_taps),
                (col_hbm, col_taps),
                (rate_hbm, rate_s),
                (off_hbm, off_v),
                (level_hbm, level_v),
                (off_hbm, off_s),
                (level_hbm, level_s),
            )
        )
    ]
    for load in small:
        load.start()
    load_target.start()
    load_dwell.wait()
    low = lanes((1, COLS)) < RIM

    def to_ring(ref, col):
        at = col - first_tile(col)

        def pick(k):
            return ref[:, pl.ds(pl.multiple_of(k * COLS, COLS), COLS)].astype(F32)

        after = jnp.where(col < n_scen - 1, pick(jnp.minimum(at + 1, 2)), 0.0)
        before = jnp.where(col > 0, pick(jnp.maximum(at - 1, 0)), 0.0)
        return pick(at), jnp.where(low, after, before)

    for g in range(4):
        upper = tile[64 * g : 64 * g + 32, :].astype(F32)
        lower = pltpu.roll(tile[64 * g + 32 : 64 * g + 64, :].astype(F32), RIM, 1)
        pack_l[32 * g : 32 * g + 32, :] = jnp.where(low, upper, lower).astype(BF16)
        pack_r[32 * g : 32 * g + 32, :] = jnp.where(low, lower, upper).astype(BF16)
    for k, col in enumerate((up_sc, down_sc)):
        load_rims[k].wait()
        own, side = to_ring(t_raw.at[k], col)
        t_send[k, :, 0:COLS] = own.astype(BF16)
        t_send[k, :, COLS:RING] = side.astype(BF16)

    @pl.when(sp == 0)
    def _():
        t_top[...] = jnp.zeros_like(t_top)
        rim_up[...] = jnp.zeros_like(rim_up)

    @pl.when(sp == n_space - 1)
    def _():
        t_bot[...] = jnp.zeros_like(t_bot)
        rim_down[...] = jnp.zeros_like(rim_down)

    def arrive(ks):
        for k in ks:
            pl.when(comes[k])(copies[k].wait_recv)

    side_ok = jnp.where(lanes((1, COLS)) < RIM, jnp.where(has_right, 1, 0), jnp.where(has_left, 1, 0)) > 0
    low = lanes((1, COLS)) < RIM

    for load in small:
        load.wait()

    taps8[...] = jnp.zeros_like(taps8)
    taps8[0:NRATE, 0:TAPS] = row_taps[...].astype(F32)
    taps8[4 : 4 + NRATE, 0:TAPS] = col_taps[...].astype(F32)
    taps = taps8[...]
    flip = jnp.where(
        lax.broadcasted_iota(jnp.int32, (RING, RING), 0) + lanes((RING, RING)) == TAPS - 1, 1.0, 0.0
    ).astype(BF16)
    reversed_taps = jnp.dot(taps.astype(BF16), flip, preferred_element_type=F32)

    def toeplitz(line, count_, first):
        return pltpu.roll(
            jnp.broadcast_to(line, (count_, RING)), first % RING, 1, stride=1, stride_axis=0
        )

    for q in range(NRATE):
        band = toeplitz(taps[q : q + 1], 192, 1).astype(BF16)
        row_fwd[0, 160 * q : 160 * q + 160, :] = band[0:160]
        row_fwd[1, 160 * q : 160 * q + 160, :] = band[32:192]
        band = toeplitz(taps[4 + q : 5 + q], 320, -RADIUS - 32)
        col_tall[q] = band[:, 0:COLS]
        col_mat[q] = band[32 : 32 + RING].astype(BF16)
        band = toeplitz(reversed_taps[q : q + 1], 192, 1)
        row_tall[q, 0] = band[:, 0:COLS]
        row_tall[q, 1] = band[:, COLS:RING]
        row_adj[:, RING * q : RING * q + RING] = band[0:128].astype(BF16)

    pl.semaphore_wait(barrier, greeted)

    first_rows, last_rows = slice(0, RIM), slice(ROWS - RIM, ROWS)
    own_first, own_last = tile.at[first_rows], tile.at[last_rows]
    pairs = (
        (own_first, rim_down),
        (own_last, rim_up),
        (pack_l, recv_r),
        (pack_r, recv_l),
        (pack_l.at[0:32], corners.at[3]),
        (pack_r.at[0:32], corners.at[2]),
        (pack_l.at[96:128], corners.at[1]),
        (pack_r.at[96:128], corners.at[0]),
        (t_send.at[0], t_bot),
        (t_send.at[1], t_top),
    )
    copies = [
        pltpu.make_async_remote_copy(
            src_ref=src,
            dst_ref=dst,
            send_sem=send_sem.at[k],
            recv_sem=recv_sem.at[k],
            device_id=peers[k][:2],
            device_id_type=MESH,
        )
        for k, (src, dst) in enumerate(pairs)
    ]
    for k in (8, 9, 4, 5, 6, 7, 2, 3, 0, 1):
        pl.when(peers[k][2])(copies[k].start)

    offs = off_v[...]
    row_at = sp * ROWS + lax.broadcasted_iota(jnp.int32, (OUT, SCEN), 0) - 32 + offs[0:1, :]
    row_in = jnp.where((row_at >= 0) & (row_at < n_space * ROWS), 1.0, 0.0).astype(BF16)
    ring_at = lax.broadcasted_iota(jnp.int32, (RING, SCEN), 0)
    col_at = jnp.where(ring_at < COLS + RIM, ring_at, ring_at - RING) + sc * COLS + offs[1:2, :]
    col_in = jnp.where((col_at >= 0) & (col_at < n_scen * COLS), 1.0, 0.0)
    levels = level_v[...]
    for q in range(NRATE):
        mine = jnp.where(levels == q, 1.0, 0.0)
        seen = lax.dot_general(
            row_in, (col_in * mine).astype(BF16), (((1,), (1,)), ((), ())), preferred_element_type=F32
        )
        rate = rate_s[q]
        count[q] = seen * (rate * rate * (1.0 / SCEN))

    load_target.wait()
    own, side = to_ring(t_own, sc)
    wide[:, 0:COLS] = own.astype(BF16)
    wide[:, COLS:RING] = side.astype(BF16)

    shift_rows = [off_s[0, s] for s in range(SCEN)]
    shift_cols = [off_s[1, s] for s in range(SCEN)]
    level_of = [level_s[0, s] for s in range(SCEN)]
    weights = [rate_s[level_of[s]] * (1.0 / SCEN) for s in range(SCEN)]

    for pair in range(SCEN // 2):
        bands = [
            col_tall[level_of[s], pl.ds(32 - shift_cols[s], RING), :].astype(BF16)
            for s in (2 * pair, 2 * pair + 1)
        ]
        both = jnp.concatenate(bands, axis=1)
        col_pair[pair] = both
        product = jnp.dot(wide[...], both, preferred_element_type=F32)
        for k in range(2):
            s = 2 * pair + k
            part = (product[:, COLS * k : COLS * k + COLS] * weights[s]).astype(BF16)
            t_back[s, RIM:256, 0:COLS] = part[0:192]
            t_back[s, 0:192, COLS:RING] = part[64:256]
            t_back[s, 0:RIM, 0:COLS] = jnp.zeros((RIM, COLS), BF16)
            t_back[s, 192:256, COLS:RING] = jnp.zeros((RIM, COLS), BF16)
            first = row_tall[level_of[s], 0, pl.ds(32 + shift_rows[s], 128), :]
            second = row_tall[level_of[s], 1, pl.ds(32 + shift_rows[s], 128), :]
            term = jnp.dot(
                jnp.concatenate([first, second], axis=1).astype(BF16), t_back[s], preferred_element_type=F32
            )
            t_grad[...] = term if s == 0 else t_grad[...] + term
            lanes_ = slice(COLS * k, COLS * k + COLS)
            rim_band[pair, 0:64, lanes_] = jnp.where(low, first[0:64], 0.0).astype(BF16)
            rim_band[pair, 64:128, lanes_] = jnp.where(low, 0.0, second[64:128]).astype(BF16)

    dwell_x[RIM : RIM + ROWS, 0:COLS] = tile[...]
    for q in range(NRATE):
        back[RING * q + 192 : RING * q + 256, COLS:RING] = jnp.zeros((64, COLS), BF16)
    for k in range(10):
        pl.when(peers[k][2])(copies[k].wait_send)
    arrive((8, 9))
    rims = jnp.concatenate([t_top[...], t_bot[...]], axis=0)
    total = jnp.zeros((128, COLS), F32)
    for pair in range(SCEN // 2):
        product = jnp.dot(rims, col_pair[pair], preferred_element_type=F32)
        parts = [
            (product[:, COLS * k : COLS * k + COLS] * weights[2 * pair + k]).astype(BF16) for k in range(2)
        ]
        total = total + jnp.dot(rim_band[pair], jnp.concatenate(parts, axis=0), preferred_element_type=F32)
    t_grad[0:64, 0:COLS] += total[0:64]
    t_grad[64:128, COLS:RING] += total[64:128]

    arrive((2, 3))
    def unpack(begin, after, before, there):
        after, before = after.astype(F32), before.astype(F32)
        upper = jnp.where(low, after, before)
        lower = pltpu.roll(jnp.where(low, before, after), RIM, 1)
        for half, x in enumerate((upper, lower)):
            kept = jnp.where(side_ok, x, 0.0)
            dwell_x[begin + 32 * half : begin + 32 * half + 32, COLS:RING] = jnp.where(there, kept, 0.0).astype(BF16)

    for g in range(4):
        rows = slice(32 * g, 32 * g + 32)
        unpack(RIM + 64 * g, recv_r[rows, :], recv_l[rows, :], True)

    arrive((0, 1))
    dwell_x[0:RIM, 0:COLS] = rim_up[...]
    dwell_x[RIM + ROWS :, 0:COLS] = rim_down[...]

    arrive((4, 5, 6, 7))

    unpack(0, corners[1], corners[0], has_up)
    unpack(RIM + ROWS, corners[3], corners[2], has_down)

    for half in range(2):
        product = jnp.dot(
            row_fwd[half], dwell_x[128 * half : 128 * half + 256, :], preferred_element_type=F32
        ).astype(BF16)
        for q in range(NRATE):
            along[q, 160 * half : 160 * half + 160, :] = product[160 * q : 160 * q + 160]

    for q in range(NRATE):
        base = lax.dot_general(
            along[q], col_mat[q], (((1,), (1,)), ((), ())), preferred_element_type=F32
        )
        misfit = (count[q] * base).astype(BF16)
        product = jnp.dot(misfit, col_mat[q, :, 0:COLS], preferred_element_type=F32).astype(BF16)
        back[RING * q : RING * q + 256, 0:COLS] = product[0:256]
        back[RING * q : RING * q + 192, COLS:RING] = product[128:OUT]

    grad = jnp.dot(row_adj[...], back[...], preferred_element_type=F32) - t_grad[...]
    load_bound.wait()
    for half in range(2):
        rows = slice(128 * half, 128 * half + 128)
        dwell = dwell_x[RIM + 128 * half : RIM + 128 * half + 128, 0:COLS].astype(F32)
        stepped = dwell - STEP_SIZE * grad[:, COLS * half : COLS * half + COLS]
        kept = jnp.where(bound_v[rows, :] == 1, jnp.maximum(stepped, 0.0), stepped)
        next_ref[rows, :] = kept.astype(BF16)


def tile_step(n_space, n_scen, dwell, target, bound, offsets, level, rates, row_kernels, col_kernels):
    offsets, level = offsets.T, level.T
    vmem = pl.BlockSpec(memory_space=pltpu.VMEM)
    far = pl.BlockSpec(memory_space=pltpu.HBM)
    return pl.pallas_call(
        functools.partial(kernel, n_space, n_scen),
        out_shape=pltpu.VMEM((ROWS, COLS), BF16),
        in_specs=[far] * 8,
        out_specs=vmem,
        scratch_shapes=[
            pltpu.VMEM((ROWS, COLS), jnp.int32),
            pltpu.SMEM((2, SCEN), jnp.int32),
            pltpu.SMEM((1, SCEN), jnp.int32),
            pltpu.SMEM((NRATE,), F32),
            pltpu.VMEM((2, SCEN), jnp.int32),
            pltpu.VMEM((1, SCEN), jnp.int32),
            pltpu.VMEM((NRATE, TAPS), BF16),
            pltpu.VMEM((NRATE, TAPS), BF16),
            pltpu.VMEM((384, RING), BF16),
            pltpu.VMEM((ROWS, COLS), BF16),
            pltpu.VMEM((RIM, COLS), BF16),
            pltpu.VMEM((RIM, COLS), BF16),
            pltpu.VMEM((128, COLS), BF16),
            pltpu.VMEM((128, COLS), BF16),
            pltpu.VMEM((128, COLS), BF16),
            pltpu.VMEM((128, COLS), BF16),
            pltpu.VMEM((4, 32, COLS), BF16),
            pltpu.VMEM((ROWS, 3 * COLS), BF16),
            pltpu.VMEM((2, RIM, 3 * COLS), BF16),
            pltpu.VMEM((2, RIM, RING), BF16),
            pltpu.VMEM((RIM, RING), BF16),
            pltpu.VMEM((RIM, RING), BF16),
            pltpu.VMEM((ROWS, RING), BF16),
            pltpu.VMEM((8, RING), F32),
            pltpu.VMEM((2, NRATE * 160, RING), BF16),
            pltpu.VMEM((NRATE, RING, RING), BF16),
            pltpu.VMEM((128, NRATE * RING), BF16),
            pltpu.VMEM((NRATE, OUT, COLS), F32),
            pltpu.VMEM((NRATE, 2, 192, COLS), F32),
            pltpu.VMEM((SCEN // 2, RING, RING), BF16),
            pltpu.VMEM((SCEN, RING, RING), BF16),
            pltpu.VMEM((128, RING), F32),
            pltpu.VMEM((NRATE, OUT, RING), F32),
            pltpu.VMEM((SCEN // 2, 128, RING), BF16),
            pltpu.VMEM((NRATE, OUT, RING), BF16),
            pltpu.VMEM((NRATE * RING, RING), BF16),
            pltpu.SemaphoreType.DMA((10,)),
            pltpu.SemaphoreType.DMA((10,)),
            pltpu.SemaphoreType.DMA((12,)),
        ],
        compiler_params=pltpu.CompilerParams(collective_id=0, vmem_limit_bytes=48 * 1024 * 1024),
    )(*(pltpu.with_memory_space_constraint(x, pltpu.HBM) for x in (dwell, target, offsets, level, rates, row_kernels, col_kernels, bound)))


def solution(mesh):
    return jax.shard_map(
        functools.partial(tile_step, mesh.shape["space"], mesh.shape["scen"]),
        mesh=mesh,
        in_specs=(P("space", "scen"), P("space", None), P("space", "scen"), P(), P(), P(), P(), P()),
        out_specs=P("space", "scen"),
        check_vma=False,
    )
```

```python
import functools

import jax
import jax.numpy as jnp
from jax import lax
from jax.experimental import pallas as pl
from jax.experimental.pallas import tpu as pltpu
from jax.sharding import PartitionSpec as P

MESH = pl.DeviceIdType.MESH
F32 = jnp.float32
BF16 = jnp.bfloat16

TAPS = 63
RADIUS = 31
ROWS = 256
COLS = 128
RIM = 64
RING = 256
OUT = 320
NRATE = 4
SCEN = 16
STEP_SIZE = 1.0


def lanes(shape):
    return lax.broadcasted_iota(jnp.int32, shape, len(shape) - 1)


def kernel(
    n_space,
    n_scen,
    dwell_hbm,
    target_hbm,
    off_hbm,
    level_hbm,
    rate_hbm,
    row_hbm,
    col_hbm,
    bound_hbm,
    next_ref,
    bound_v,
    off_s,
    level_s,
    rate_s,
    off_v,
    level_v,
    row_taps,
    col_taps,
    dwell_x,
    tile,
    rim_up,
    rim_down,
    pack_l,
    pack_r,
    recv_l,
    recv_r,
    corners,
    t_own,
    t_raw,
    t_send,
    t_top,
    t_bot,
    wide,
    taps8,
    row_fwd,
    col_mat,
    row_adj,
    col_tall,
    row_tall,
    col_pair,
    t_back,
    t_grad,
    count,
    rim_band,
    along,
    back,
    send_sem,
    recv_sem,
    load_sem,
):
    sp = lax.axis_index("space")
    sc = lax.axis_index("scen")
    up, down, left, right = sp - 1, sp + 1, sc - 1, sc + 1
    has_up, has_down = sp > 0, sp < n_space - 1
    has_left, has_right = sc > 0, sc < n_scen - 1
    core = sp % 2
    other = (sc + n_scen // 2) % n_scen
    up_sc = jnp.where(core == 0, other, sc)
    down_sc = jnp.where(core == 0, sc, other)

    def first_tile(c):
        return jnp.minimum(jnp.maximum(c - 1, 0), n_scen - 3)

    def window(c):
        return pl.ds(pl.multiple_of(first_tile(c) * COLS, COLS), 3 * COLS)

    peers = (
        (up, sc, has_up),
        (down, sc, has_down),
        (sp, left, has_left),
        (sp, right, has_right),
        (up, left, has_up & has_left),
        (up, right, has_up & has_right),
        (down, left, has_down & has_left),
        (down, right, has_down & has_right),
        (up, up_sc, has_up),
        (down, down_sc, has_down),
    )
    comes = [peers[k][2] for k in (1, 0, 3, 2, 7, 6, 5, 4, 9, 8)]
    barrier = pltpu.get_barrier_semaphore()
    for row, col, there in [peers[k] for k in (4, 5, 6, 7, 0, 1, 8, 9, 2, 3)]:

        @pl.when(there)
        def _(row=row, col=col):
            pl.semaphore_signal(barrier, inc=1, device_id=(row, col), device_id_type=MESH)

    greeted = sum(jnp.where(there, 1, 0) for _, _, there in peers)

    load_dwell = pltpu.make_async_copy(
        dwell_hbm, tile, load_sem.at[0]
    )
    load_target = pltpu.make_async_copy(target_hbm.at[:, window(sc)], t_own, load_sem.at[1])
    load_rims = [
        pltpu.make_async_copy(
            target_hbm.at[slice(begin, begin + RIM), window(col)], t_raw.at[k], load_sem.at[10 + k]
        )
        for k, (begin, col) in enumerate(((0, up_sc), (ROWS - RIM, down_sc)))
    ]
    load_dwell.start()
    for load in load_rims:
        load.start()
    load_bound = pltpu.make_async_copy(bound_hbm, bound_v, load_sem.at[9])
    load_bound.start()
    small = [
        pltpu.make_async_copy(src, dst, load_sem.at[2 + k])
        for k, (src, dst) in enumerate(
            (
                (row_hbm, row_taps),
                (col_hbm, col_taps),
                (rate_hbm, rate_s),
                (off_hbm, off_v),
                (level_hbm, level_v),
                (off_hbm, off_s),
                (level_hbm, level_s),
            )
        )
    ]
    for load in small:
        load.start()
    load_target.start()
    load_dwell.wait()
    low = lanes((1, COLS)) < RIM

    def to_ring(ref, col):
        at = col - first_tile(col)

        def pick(k):
            return ref[:, pl.ds(pl.multiple_of(k * COLS, COLS), COLS)].astype(F32)

        after = jnp.where(col < n_scen - 1, pick(jnp.minimum(at + 1, 2)), 0.0)
        before = jnp.where(col > 0, pick(jnp.maximum(at - 1, 0)), 0.0)
        return pick(at), jnp.where(low, after, before)

    for g in range(4):
        upper = tile[64 * g : 64 * g + 32, :].astype(F32)
        lower = pltpu.roll(tile[64 * g + 32 : 64 * g + 64, :].astype(F32), RIM, 1)
        pack_l[32 * g : 32 * g + 32, :] = jnp.where(low, upper, lower).astype(BF16)
        pack_r[32 * g : 32 * g + 32, :] = jnp.where(low, lower, upper).astype(BF16)
    for k, col in enumerate((up_sc, down_sc)):
        load_rims[k].wait()
        own, side = to_ring(t_raw.at[k], col)
        t_send[k, :, 0:COLS] = own.astype(BF16)
        t_send[k, :, COLS:RING] = side.astype(BF16)

    @pl.when(sp == 0)
    def _():
        t_top[...] = jnp.zeros_like(t_top)
        rim_up[...] = jnp.zeros_like(rim_up)
        corners[0:2] = jnp.zeros((2, 32, COLS), BF16)

    @pl.when(sp == n_space - 1)
    def _():
        t_bot[...] = jnp.zeros_like(t_bot)
        rim_down[...] = jnp.zeros_like(rim_down)
        corners[2:4] = jnp.zeros((2, 32, COLS), BF16)

    @pl.when(sc == 0)
    def _():
        recv_l[...] = jnp.zeros_like(recv_l)
        for k in (0, 2):
            corners[k] = jnp.zeros((32, COLS), BF16)

    @pl.when(sc == n_scen - 1)
    def _():
        recv_r[...] = jnp.zeros_like(recv_r)
        for k in (1, 3):
            corners[k] = jnp.zeros((32, COLS), BF16)

    def arrive(ks):
        for k in ks:
            pl.when(comes[k])(copies[k].wait_recv)

    low = lanes((1, COLS)) < RIM

    for load in small:
        load.wait()

    taps8[...] = jnp.zeros_like(taps8)
    taps8[0:NRATE, 0:TAPS] = row_taps[...].astype(F32)
    taps8[4 : 4 + NRATE, 0:TAPS] = col_taps[...].astype(F32)
    taps = taps8[...]
    flip = jnp.where(
        lax.broadcasted_iota(jnp.int32, (RING, RING), 0) + lanes((RING, RING)) == TAPS - 1, 1.0, 0.0
    ).astype(BF16)
    reversed_taps = jnp.dot(taps.astype(BF16), flip, preferred_element_type=F32)

    def toeplitz(line, count_, first):
        return pltpu.roll(
            jnp.broadcast_to(line, (count_, RING)), first % RING, 1, stride=1, stride_axis=0
        )

    for q in range(NRATE):
        band = toeplitz(taps[q : q + 1], 192, 1).astype(BF16)
        row_fwd[0, 160 * q : 160 * q + 160, :] = band[0:160]
        row_fwd[1, 160 * q : 160 * q + 160, :] = band[32:192]
        band = toeplitz(taps[4 + q : 5 + q], 320, -RADIUS - 32)
        col_tall[q] = band[:, 0:COLS]
        col_mat[q] = band[32 : 32 + RING].astype(BF16)
        band = toeplitz(reversed_taps[q : q + 1], 192, 1)
        row_tall[q, 0] = band[:, 0:COLS]
        row_tall[q, 1] = band[:, COLS:RING]
        row_adj[:, RING * q : RING * q + RING] = band[0:128].astype(BF16)

    pl.semaphore_wait(barrier, greeted)

    first_rows, last_rows = slice(0, RIM), slice(ROWS - RIM, ROWS)
    own_first, own_last = tile.at[first_rows], tile.at[last_rows]
    pairs = (
        (own_first, rim_down),
        (own_last, rim_up),
        (pack_l, recv_r),
        (pack_r, recv_l),
        (pack_l.at[0:32], corners.at[3]),
        (pack_r.at[0:32], corners.at[2]),
        (pack_l.at[96:128], corners.at[1]),
        (pack_r.at[96:128], corners.at[0]),
        (t_send.at[0], t_bot),
        (t_send.at[1], t_top),
    )
    copies = [
        pltpu.make_async_remote_copy(
            src_ref=src,
            dst_ref=dst,
            send_sem=send_sem.at[k],
            recv_sem=recv_sem.at[k],
            device_id=peers[k][:2],
            device_id_type=MESH,
        )
        for k, (src, dst) in enumerate(pairs)
    ]
    for k in (8, 9, 4, 5, 6, 7, 2, 3, 0, 1):
        pl.when(peers[k][2])(copies[k].start)

    offs = off_v[...]
    row_at = sp * ROWS + lax.broadcasted_iota(jnp.int32, (OUT, SCEN), 0) - 32 + offs[0:1, :]
    row_in = jnp.where((row_at >= 0) & (row_at < n_space * ROWS), 1.0, 0.0).astype(BF16)
    ring_at = lax.broadcasted_iota(jnp.int32, (RING, SCEN), 0)
    col_at = jnp.where(ring_at < COLS + RIM, ring_at, ring_at - RING) + sc * COLS + offs[1:2, :]
    col_in = jnp.where((col_at >= 0) & (col_at < n_scen * COLS), 1.0, 0.0)
    levels = level_v[...]
    for q in range(NRATE):
        mine = jnp.where(levels == q, 1.0, 0.0)
        seen = lax.dot_general(
            row_in, (col_in * mine).astype(BF16), (((1,), (1,)), ((), ())), preferred_element_type=F32
        )
        rate = rate_s[q]
        count[q] = seen * (rate * rate * (1.0 / SCEN))

    load_target.wait()
    own, side = to_ring(t_own, sc)
    wide[:, 0:COLS] = own.astype(BF16)
    wide[:, COLS:RING] = side.astype(BF16)

    shift_rows = [off_s[0, s] for s in range(SCEN)]
    shift_cols = [off_s[1, s] for s in range(SCEN)]
    level_of = [level_s[0, s] for s in range(SCEN)]
    weights = [rate_s[level_of[s]] * (1.0 / SCEN) for s in range(SCEN)]

    for pair in range(SCEN // 2):
        bands = [
            col_tall[level_of[s], pl.ds(32 - shift_cols[s], RING), :].astype(BF16)
            for s in (2 * pair, 2 * pair + 1)
        ]
        both = jnp.concatenate(bands, axis=1)
        col_pair[pair] = both
        product = jnp.dot(wide[...], both, preferred_element_type=F32)
        for k in range(2):
            s = 2 * pair + k
            part = (product[:, COLS * k : COLS * k + COLS] * weights[s]).astype(BF16)
            t_back[s, RIM:256, 0:COLS] = part[0:192]
            t_back[s, 0:192, COLS:RING] = part[64:256]
            t_back[s, 0:RIM, 0:COLS] = jnp.zeros((RIM, COLS), BF16)
            t_back[s, 192:256, COLS:RING] = jnp.zeros((RIM, COLS), BF16)
            first = row_tall[level_of[s], 0, pl.ds(32 + shift_rows[s], 128), :]
            second = row_tall[level_of[s], 1, pl.ds(32 + shift_rows[s], 128), :]
            term = jnp.dot(
                jnp.concatenate([first, second], axis=1).astype(BF16), t_back[s], preferred_element_type=F32
            )
            t_grad[...] = term if s == 0 else t_grad[...] + term
            lanes_ = slice(COLS * k, COLS * k + COLS)
            rim_band[pair, 0:64, lanes_] = jnp.where(low, first[0:64], 0.0).astype(BF16)
            rim_band[pair, 64:128, lanes_] = jnp.where(low, 0.0, second[64:128]).astype(BF16)

    dwell_x[RIM : RIM + ROWS, 0:COLS] = tile[...]
    for q in range(NRATE):
        back[RING * q + 192 : RING * q + 256, COLS:RING] = jnp.zeros((64, COLS), BF16)
    for k in range(10):
        pl.when(peers[k][2])(copies[k].wait_send)
    arrive((8, 9))
    rims = jnp.concatenate([t_top[...], t_bot[...]], axis=0)
    total = jnp.zeros((128, COLS), F32)
    for pair in range(SCEN // 2):
        product = jnp.dot(rims, col_pair[pair], preferred_element_type=F32)
        parts = [
            (product[:, COLS * k : COLS * k + COLS] * weights[2 * pair + k]).astype(BF16) for k in range(2)
        ]
        total = total + jnp.dot(rim_band[pair], jnp.concatenate(parts, axis=0), preferred_element_type=F32)
    t_grad[0:64, 0:COLS] += total[0:64]
    t_grad[64:128, COLS:RING] += total[64:128]

    arrive((2, 3))
    def unpack(begin, after, before):
        after, before = after.astype(F32), before.astype(F32)
        upper = jnp.where(low, after, before)
        lower = pltpu.roll(jnp.where(low, before, after), RIM, 1)
        for half, x in enumerate((upper, lower)):
            dwell_x[begin + 32 * half : begin + 32 * half + 32, COLS:RING] = x.astype(BF16)

    for g in range(4):
        rows = slice(32 * g, 32 * g + 32)
        unpack(RIM + 64 * g, recv_r[rows, :], recv_l[rows, :])

    arrive((0, 1))
    dwell_x[0:RIM, 0:COLS] = rim_up[...]
    dwell_x[RIM + ROWS :, 0:COLS] = rim_down[...]

    arrive((4, 5, 6, 7))

    unpack(0, corners[1], corners[0])
    unpack(RIM + ROWS, corners[3], corners[2])

    for half in range(2):
        product = jnp.dot(
            row_fwd[half], dwell_x[128 * half : 128 * half + 256, :], preferred_element_type=F32
        ).astype(BF16)
        for q in range(NRATE):
            along[q, 160 * half : 160 * half + 160, :] = product[160 * q : 160 * q + 160]

    for q in range(NRATE):
        base = lax.dot_general(
            along[q], col_mat[q], (((1,), (1,)), ((), ())), preferred_element_type=F32
        )
        misfit = (count[q] * base).astype(BF16)
        product = jnp.dot(misfit, col_mat[q, :, 0:COLS], preferred_element_type=F32).astype(BF16)
        back[RING * q : RING * q + 256, 0:COLS] = product[0:256]
        back[RING * q : RING * q + 192, COLS:RING] = product[128:OUT]

    grad = jnp.dot(row_adj[...], back[...], preferred_element_type=F32) - t_grad[...]
    load_bound.wait()
    for half in range(2):
        rows = slice(128 * half, 128 * half + 128)
        dwell = dwell_x[RIM + 128 * half : RIM + 128 * half + 128, 0:COLS].astype(F32)
        stepped = dwell - STEP_SIZE * grad[:, COLS * half : COLS * half + COLS]
        kept = jnp.where(bound_v[rows, :] == 1, jnp.maximum(stepped, 0.0), stepped)
        next_ref[rows, :] = kept.astype(BF16)


def tile_step(n_space, n_scen, dwell, target, bound, offsets, level, rates, row_kernels, col_kernels):
    offsets, level = offsets.T, level.T
    vmem = pl.BlockSpec(memory_space=pltpu.VMEM)
    far = pl.BlockSpec(memory_space=pltpu.HBM)
    return pl.pallas_call(
        functools.partial(kernel, n_space, n_scen),
        out_shape=pltpu.VMEM((ROWS, COLS), BF16),
        in_specs=[far] * 8,
        out_specs=vmem,
        scratch_shapes=[
            pltpu.VMEM((ROWS, COLS), jnp.int32),
            pltpu.SMEM((2, SCEN), jnp.int32),
            pltpu.SMEM((1, SCEN), jnp.int32),
            pltpu.SMEM((NRATE,), F32),
            pltpu.VMEM((2, SCEN), jnp.int32),
            pltpu.VMEM((1, SCEN), jnp.int32),
            pltpu.VMEM((NRATE, TAPS), BF16),
            pltpu.VMEM((NRATE, TAPS), BF16),
            pltpu.VMEM((384, RING), BF16),
            pltpu.VMEM((ROWS, COLS), BF16),
            pltpu.VMEM((RIM, COLS), BF16),
            pltpu.VMEM((RIM, COLS), BF16),
            pltpu.VMEM((128, COLS), BF16),
            pltpu.VMEM((128, COLS), BF16),
            pltpu.VMEM((128, COLS), BF16),
            pltpu.VMEM((128, COLS), BF16),
            pltpu.VMEM((4, 32, COLS), BF16),
            pltpu.VMEM((ROWS, 3 * COLS), BF16),
            pltpu.VMEM((2, RIM, 3 * COLS), BF16),
            pltpu.VMEM((2, RIM, RING), BF16),
            pltpu.VMEM((RIM, RING), BF16),
            pltpu.VMEM((RIM, RING), BF16),
            pltpu.VMEM((ROWS, RING), BF16),
            pltpu.VMEM((8, RING), F32),
            pltpu.VMEM((2, NRATE * 160, RING), BF16),
            pltpu.VMEM((NRATE, RING, RING), BF16),
            pltpu.VMEM((128, NRATE * RING), BF16),
            pltpu.VMEM((NRATE, OUT, COLS), F32),
            pltpu.VMEM((NRATE, 2, 192, COLS), F32),
            pltpu.VMEM((SCEN // 2, RING, RING), BF16),
            pltpu.VMEM((SCEN, RING, RING), BF16),
            pltpu.VMEM((128, RING), F32),
            pltpu.VMEM((NRATE, OUT, RING), F32),
            pltpu.VMEM((SCEN // 2, 128, RING), BF16),
            pltpu.VMEM((NRATE, OUT, RING), BF16),
            pltpu.VMEM((NRATE * RING, RING), BF16),
            pltpu.SemaphoreType.DMA((10,)),
            pltpu.SemaphoreType.DMA((10,)),
            pltpu.SemaphoreType.DMA((12,)),
        ],
        compiler_params=pltpu.CompilerParams(collective_id=0, vmem_limit_bytes=48 * 1024 * 1024),
    )(*(pltpu.with_memory_space_constraint(x, pltpu.HBM) for x in (dwell, target, offsets, level, rates, row_kernels, col_kernels, bound)))


def solution(mesh):
    return jax.shard_map(
        functools.partial(tile_step, mesh.shape["space"], mesh.shape["scen"]),
        mesh=mesh,
        in_specs=(P("space", "scen"), P("space", None), P("space", "scen"), P(), P(), P(), P(), P()),
        out_specs=P("space", "scen"),
        check_vma=False,
    )
```
